512 devices in a mesh: group: 16 (over z, core), dp: 32 (over x, y).
Axes of the slice: x: 4, y: 8, z: 8, core: 2. Of those that a mesh axis runs over, the one named last changes fastest.
Arguments:
- queries: bfloat16 [1024, 128, 512], P(('group', 'dp')), may hold values from -256 to 256
- passages: bfloat16 [3072, 128, 512], P(('group', 'dp')), may hold values from -6 to 6
- candidates: int32 [1024, 16], replicated, may hold values from 0 to 3071, as said below
- positives: int32 [1024, 128], P(('group', 'dp')), may hold values from 0 to 2047
- row_weight: float32 [1024, 128], P(('group', 'dp')), may hold values from 0.25 to 4
- owner_map: int32 [3072], replicated, may hold values from 0 to 3071, as said below
Outputs:
- grad_query: bfloat16 [1024, 128, 512], P(('group', 'dp'))
- grad_passage: bfloat16 [3072, 128, 512], P(('group', 'dp'))
The draws below stay inside these ranges and needn't reach their ends.
Inputs may be any that keep to these rules, and one draw needn't show every extreme that they name: `owner_map`: A permutation: entry i is the row block of passages that holds block id i. `candidates`: each row lists 16 different block ids: 12 held by devices of the query block's own group, the others held by devices of other groups with the same dp index. Over all query blocks of one device, at most 1 distinct listed blocks lie on any one device of its group and at most 1 on the devices of any one other group; for every device both bounds are reached.
All inputs are finite; a program needn't handle non-finite values.
Results may differ from the reference program's by a relative error of at most 0.0057.
Values may be sent and summed in bfloat16 or wider, within the bound.
A program may use at most 128 MiB of HBM per device.

```python
import math
import jax
import jax.numpy as jnp
from jax import lax

D = 512
BR = 128
NCAND = 16
NLOCAL = 12
QB_DEV = 2
PB_DEV = 6
NREMOTE = 4
CAPL = 1
CAPR = 1
QBLOCKS = 1024
NBLK = 3072
N_GROUP = 16
N_DP = 32
DEVICES = 512


def routing_tables(key):
    owner_map = jax.random.permutation(jax.random.fold_in(key, 7), NBLK).astype(jnp.int32)
    block_at = jnp.argsort(owner_map).astype(jnp.int32)
    hot_peer = jax.random.randint(jax.random.fold_in(key, 8), (N_GROUP,), 0, N_DP)
    local_peer = jnp.repeat(jnp.arange(N_DP, dtype=jnp.int32), CAPL)
    remote_group = jnp.repeat(jnp.arange(N_GROUP, dtype=jnp.int32), CAPR)

    def one_device(device):
        device_key = jax.random.fold_in(jax.random.fold_in(key, 9), device)
        group_index = device // N_DP
        column = device % N_DP
        local_rank = jax.random.randint(jax.random.fold_in(device_key, 1), (N_DP, PB_DEV), 0, 65536) * PB_DEV + jnp.arange(PB_DEV, dtype=jnp.int32)[None, :]
        local_slot = jnp.argsort(local_rank, axis=1)[:, :CAPL].astype(jnp.int32)
        remote_rank = jax.random.randint(jax.random.fold_in(device_key, 2), (N_GROUP, PB_DEV), 0, 65536) * PB_DEV + jnp.arange(PB_DEV, dtype=jnp.int32)[None, :]
        remote_slot = jnp.argsort(remote_rank, axis=1)[:, :CAPR].astype(jnp.int32)
        local_pos = ((group_index * N_DP + jnp.arange(N_DP, dtype=jnp.int32))[:, None] * PB_DEV + local_slot).reshape(-1)
        remote_pos = ((jnp.arange(N_GROUP, dtype=jnp.int32) * N_DP + column)[:, None] * PB_DEV + remote_slot).reshape(-1)
        hot_remote = (group_index + 1 + jax.random.randint(jax.random.fold_in(device_key, 3), (), 0, N_GROUP - 1)) % N_GROUP

        def one_block(block):
            block_key = jax.random.fold_in(device_key, 100 + block)
            local_score = jax.random.randint(jax.random.fold_in(block_key, 1), (N_DP * CAPL,), 0, 65536) * 1024 + jnp.arange(N_DP * CAPL, dtype=jnp.int32)
            local_score = local_score + jnp.where(local_peer == hot_peer[group_index], 134217728, 0)
            pick_local = jnp.argsort(-local_score)[:NLOCAL]
            remote_score = jax.random.randint(jax.random.fold_in(block_key, 2), (N_GROUP * CAPR,), 0, 65536) * 1024 + jnp.arange(N_GROUP * CAPR, dtype=jnp.int32)
            remote_score = remote_score + jnp.where(remote_group == hot_remote, 134217728, 0)
            remote_score = jnp.where(remote_group == group_index, -1, remote_score)
            pick_remote = jnp.argsort(-remote_score)[:NREMOTE]
            chosen = jnp.concatenate([local_pos[pick_local], remote_pos[pick_remote]])
            shuffle = jax.random.permutation(jax.random.fold_in(block_key, 3), NCAND)
            return block_at[chosen[shuffle]]
        return jax.vmap(one_block)(jnp.arange(QB_DEV, dtype=jnp.int32))
    lists = jax.vmap(one_device)(jnp.arange(DEVICES, dtype=jnp.int32))
    return (owner_map, lists.reshape(QBLOCKS, NCAND).astype(jnp.int32))


def draw_owner_map(key, part):
    return routing_tables(key)[0]


def draw_candidates(key, part):
    return routing_tables(key)[1]


def draw_queries(key, part):
    values = jax.random.truncated_normal(jax.random.fold_in(key, 1), -6.0, 6.0, (QBLOCKS, BR, D), jnp.float32)
    return values.astype(jnp.bfloat16)


def with_ends(entries, own_key, low, top_value):
    spot = [jax.random.randint(jax.random.fold_in(own_key, axis), (), 0, length) for axis, length in enumerate(entries.shape)]
    main_axis = entries.shape.index(max(entries.shape))
    beside = spot[:main_axis] + [(spot[main_axis] + 1) % entries.shape[main_axis]] + spot[main_axis + 1:]
    return entries.at[tuple(spot)].set(low).at[tuple(beside)].set(top_value)


def block_scale(own_key, extent, cuts, low, largest):
    gain, own = 1.0, jax.random.fold_in(own_key, 6)
    for position, blocks in cuts:
        draws = jnp.exp(jax.random.uniform(jax.random.fold_in(own, position), (blocks,), jnp.float32, low / len(cuts), largest / len(cuts)))
        gain = gain * jnp.repeat(draws, extent[position] // blocks).reshape([-1 if axis == position else 1 for axis in range(len(extent))])
    return gain


def normal_values(own_key, dims, scale, bound, shards=(), kind=jnp.bfloat16):
    values = jax.random.normal(own_key, dims, jnp.float32) * scale
    if len(shards) > 0:
        values = block_scale(own_key, dims, shards, -0.22, 0.18) * values
    return jnp.clip(values, min=-bound, max=bound).astype(kind)


def setup_inputs(seed: int = 0) -> dict:
    key_of = jax.random.split(jax.random.key(seed), 7)
    return {
        "queries": draw_queries(jax.random.fold_in(key_of[6], 71), 0),
        "passages": normal_values(key_of[1], (NBLK, BR, D), 1.0, 6.0, ((0, 512),)),
        "candidates": draw_candidates(jax.random.fold_in(key_of[6], 71), 0),
        "positives": with_ends(jax.random.randint(key_of[3], (QBLOCKS, BR), 0, NCAND * BR), jax.random.fold_in(key_of[3], 1), 0, (NCAND * BR) - 1).astype(jnp.int32),
        "row_weight": jnp.clip(jnp.exp(math.log(4.0) - 2.7725887 * jax.random.uniform(key_of[4], (QBLOCKS, BR), jnp.float32) ** block_scale(key_of[4], (QBLOCKS, BR), ((0, 512),), -0.2, 0.2)), 0.25, 4.0),
        "owner_map": draw_owner_map(jax.random.fold_in(key_of[6], 71), 0),
    }


def reference(queries, passages, candidates, positives, row_weight, owner_map):
    score_scale = 3.0 / math.sqrt(D)
    listing = jnp.arange(QB_DEV * NCAND, dtype=jnp.int32)
    target_index = jnp.arange(NCAND * BR, dtype=jnp.int32)

    def device_step(grad_sum, device):
        start = (device * QB_DEV).astype(jnp.int32)
        query_part = lax.dynamic_slice_in_dim(queries, start, QB_DEV, 0).astype(jnp.float32)
        listed = lax.dynamic_slice_in_dim(candidates, start, QB_DEV, 0)
        target_rows = lax.dynamic_slice_in_dim(positives, start, QB_DEV, 0)
        weight_rows = lax.dynamic_slice_in_dim(row_weight, start, QB_DEV, 0)
        positions = jnp.take(owner_map, listed.reshape(-1)).astype(jnp.int32)
        candidate = jnp.take(passages, positions, axis=0).astype(jnp.float32).reshape(QB_DEV, NCAND, BR, D)
        scores = jnp.einsum('brd,bkjd->brkj', query_part, candidate) * score_scale
        probability = jax.nn.softmax(scores.reshape(QB_DEV, BR, NCAND * BR), axis=-1)
        target = (target_index[None, None, :] == target_rows[:, :, None]).astype(jnp.float32)
        dscore = ((probability - target) * (weight_rows[:, :, None] * score_scale)).astype(jnp.bfloat16)
        dscore = lax.optimization_barrier(dscore).astype(jnp.float32).reshape(QB_DEV, BR, NCAND, BR)
        grad_query = jnp.einsum('brkj,bkjd->brd', dscore, candidate).astype(jnp.bfloat16)
        pair_terms = jnp.einsum('brkj,brd->bkjd', dscore, query_part).reshape(QB_DEV * NCAND, BR, D)
        same_block = positions[:, None] == positions[None, :]
        merged = jnp.einsum('lm,mxd->lxd', same_block.astype(jnp.float32), pair_terms, precision=lax.Precision.HIGHEST)
        rounded = lax.optimization_barrier(merged.astype(jnp.bfloat16)).astype(jnp.float32)
        earlier = same_block & (listing[None, :] < listing[:, None])
        unique = jnp.logical_not(jnp.any(earlier, axis=1)).astype(jnp.float32)
        grad_sum = grad_sum.at[positions].add(rounded * unique[:, None, None])
        return (grad_sum, grad_query)
    grad_sum, grad_query = lax.scan(device_step, jnp.zeros((NBLK, BR, D), jnp.float32), jnp.arange(DEVICES, dtype=jnp.int32))
    return (grad_query.reshape(QBLOCKS, BR, D), grad_sum.astype(jnp.bfloat16))
```

```python
import functools
import math

import jax
import jax.numpy as jnp
from jax import lax
from jax.experimental import pallas as pl
from jax.experimental.pallas import tpu as pltpu
from jax.sharding import PartitionSpec as P

MESH = pl.DeviceIdType.MESH
NEG = -1e30
CORES = 2
SIZES = (4, 8)


def scratch_plan(nx, ny, nz, qb, owned, rows, width):
    lanes = qb * rows
    dma = pltpu.SemaphoreType.DMA
    bf, f32 = jnp.bfloat16, jnp.float32
    hy, hz, hx = max(ny // 2, 1), max(nz // 2, 1), max(nx // 2, 1)
    plan = {
        "qy": pltpu.VMEM((ny, lanes, width), bf),
        "qz": pltpu.VMEM((nz, lanes, width), bf),
        "pc": pltpu.VMEM((owned, rows, width), bf),
        "tab": pltpu.SMEM(((nx * ny + CORES * nz) * 3,), jnp.int32),
        "auxy": pltpu.VMEM((ny, 8, lanes), f32),
        "auxz": pltpu.VMEM((nz, 8, lanes), f32),
        "e": pltpu.VMEM((nx * ny + CORES * nz, rows, lanes), f32),
        "d": pltpu.VMEM((nx * ny + CORES * nz, rows, lanes), bf),
        "my": pltpu.VMEM((nx, ny, lanes), f32),
        "sy": pltpu.VMEM((nx, ny, lanes), f32),
        "mz": pltpu.VMEM((CORES, nz, lanes), f32),
        "sz": pltpu.VMEM((CORES, nz, lanes), f32),
        "zst": pltpu.VMEM((nz, lanes), f32),
        "zsr": pltpu.VMEM((nz, nz, lanes), f32),
        "yst": pltpu.VMEM((ny, lanes), f32),
        "ysr": pltpu.VMEM((ny, ny, lanes), f32),
        "ya": pltpu.VMEM((ny, lanes), f32),
        "fin": pltpu.VMEM((8, lanes), f32),
        "zfr": pltpu.VMEM((nz, 8, lanes), f32),
        "t": pltpu.VMEM((max(ny, nz), rows, width), f32),
        "gqy": pltpu.VMEM((ny, lanes, width), f32),
        "gqz": pltpu.VMEM((nz, lanes, width), f32),
        "gp": pltpu.VMEM((nx + CORES, owned, rows, width), f32),
        "yo": pltpu.VMEM((2, hy, qb, rows, width), bf),
        "yi": pltpu.VMEM((2, hy, qb, rows, width), bf),
        "zo": pltpu.VMEM((2, hz, qb, rows, width), bf),
        "zi": pltpu.VMEM((2, hz, qb, rows, width), bf),
        "xo": pltpu.VMEM((2, hx, owned, rows, width), bf),
        "xi": pltpu.VMEM((2, hx, owned, rows, width), bf),
        "co": pltpu.VMEM((owned, rows, width), bf),
        "ci": pltpu.VMEM((owned, rows, width), bf),
        "ys_s": dma((2, hy, qb)),
        "ys_r": dma((ny, qb)),
        "zs_s": dma((2, hz, qb)),
        "zs_r": dma((nz, qb)),
        "xs_s": dma((2, hx, owned)),
        "xs_r": dma((nx, owned)),
        "cs": dma((4,)),
        "ay_s": dma((ny,)),
        "ay_r": dma((ny,)),
        "az_s": dma((nz,)),
        "az_r": dma((nz,)),
        "ty_s": dma((ny,)),
        "ty_r": dma((ny,)),
        "tz_s": dma((nz,)),
        "tz_r": dma((nz,)),
        "fz_s": dma((nz,)),
        "fz_r": dma((nz,)),
        "ry_s": dma((2, hy, qb)),
        "ry_r": dma((2, hy, qb)),
        "rz_s": dma((2, hz, qb)),
        "rz_r": dma((2, hz, qb)),
        "rx_s": dma((2, hx, owned)),
        "rx_r": dma((2, hx, owned)),
    }
    for h in range(1, nx):
        plan[f"px{h}"] = pltpu.VMEM((owned, rows, width), bf)
    return plan


def kernel(sizes, names, q_ref, p_ref, cand_ref, own_ref, pos_ref, w_ref, gq_ref, gp_ref, *scratch):
    nx, ny, nz = sizes
    s = dict(zip(names, scratch))
    qb, rows, width = q_ref.shape
    owned = p_ref.shape[0]
    ncand = cand_ref.shape[0]
    lanes = qb * rows
    scale = 3.0 / math.sqrt(width)
    dp_size = nx * ny
    g, dp = lax.axis_index("group"), lax.axis_index("dp")
    x, y = dp // ny, dp % ny
    z, c = g // CORES, g % CORES

    def at_y(r):
        return (g, x * ny + (y + r) % ny)

    def at_x(r):
        return (g, ((x + r) % nx) * ny + y)

    def at_z(r):
        return (((z + r) % nz) * CORES + c, dp)

    partner = (z * CORES + (1 - c), dp)

    tile_row = lax.broadcasted_iota(jnp.int32, (8, lanes), 0)
    w_row = jnp.concatenate([w_ref[b : b + 1, :] for b in range(qb)], axis=1) * scale
    pos_row = jnp.concatenate([pos_ref[b : b + 1, :] for b in range(qb)], axis=1).astype(jnp.float32)
    own_aux = jnp.where(tile_row == 0, w_row, jnp.where(tile_row == 1, pos_row, 0.0))
    s["auxy"][0] = own_aux
    s["auxz"][0] = own_aux

    peers = [at_y(r) for r in range(1, ny)] + [at_z(r) for r in range(1, nz)] + [partner]
    peers += [at_x(r) for r in sorted({1 % nx, (nx - 1) % nx} - {0})]
    barrier = pltpu.get_barrier_semaphore()
    for peer in peers:
        pl.semaphore_signal(barrier, inc=1, device_id=peer, device_id_type=MESH)
    pl.semaphore_wait(barrier, len(peers))

    started = []

    def send(src, dst, send_sem, recv_sem, device):
        return pltpu.make_async_remote_copy(
            src_ref=src, dst_ref=dst, send_sem=send_sem, recv_sem=recv_sem, device_id=device, device_id_type=MESH
        )

    def start(copy):
        copy.start()
        started.append(copy)

    def line_steps(n, parts, t):
        half = n // 2
        if t < half - 1:
            return [(way, part) for part in range(parts) for way in (0, 1)]
        return [(way, part) for part in range(parts) for way in (0, 1) if (part >= parts // 2) == (way == 1)]

    def slots(n, way, t):
        return ((-t) % n, (-(t + 1)) % n) if way == 0 else (t, t + 1)

    def query_copy(line, n, device_at, way, t, part):
        src, dst = slots(n, way, t)
        buf = s["q" + line]
        block = pl.ds(part * rows, rows)
        return send(
            q_ref.at[part] if t == 0 else buf.at[src, block],
            buf.at[dst, block],
            s[line + "s_s"].at[way, t, part],
            s[line + "s_r"].at[dst, part],
            device_at(1 if way == 0 else n - 1),
        )

    def y_copy(way, t, part):
        return query_copy("y", ny, at_y, way, t, part)

    def z_copy(way, t, part):
        return query_copy("z", nz, at_z, way, t, part)

    passages = [p_ref] + [s[f"px{h}"] for h in range(1, nx)] + [s["pc"]]

    def x_copy(way, t, part):
        src, dst = slots(nx, way, t)
        return send(
            passages[src].at[part],
            passages[dst].at[part],
            s["xs_s"].at[way, t, part],
            s["xs_r"].at[dst, part],
            at_x(1 if way == 0 else nx - 1),
        )

    if ny > 1:
        for way, part in line_steps(ny, qb, 0):
            start(y_copy(way, 0, part))
    if nz > 1:
        for way, part in line_steps(nz, qb, 0):
            start(z_copy(way, 0, part))
    first = sorted(line_steps(nx, owned, 0), key=lambda e: (e[1] + (owned // 2 if e[0] else 0)) % owned)
    for way, part in first:
        start(x_copy(way, 0, part))
    core_gather = send(p_ref, s["pc"], s["cs"].at[0], s["cs"].at[1], partner)
    start(core_gather)

    def spread(name, n, device_at, src, dst, sems):
        copies = [
            send(src, dst.at[n - r], s[sems + "_s"].at[r], s[sems + "_r"].at[n - r], device_at(r)) for r in range(1, n)
        ]
        for copy in copies:
            start(copy)
        return copies

    aux_y = spread("aux", ny, at_y, s["auxy"].at[0], s["auxy"], "ay")
    aux_z = spread("aux", nz, at_z, s["auxz"].at[0], s["auxz"], "az")

    def entry_y(h, r):
        return (h * ny + r) * 3

    def entry_z(h, r):
        return (nx * ny + h * nz + r) * 3

    def fill(lister, holders, entries):
        found = [jnp.int32(0)] * len(holders)
        for b in range(qb):
            listing = [jnp.int32(-1)] * len(holders)
            for k in range(ncand):
                place = own_ref[cand_ref[k, lister * qb + b]]
                for i, holder in enumerate(holders):
                    offset = place - holder * owned
                    hit = (offset >= 0) & (offset < owned)
                    listing[i] = jnp.where(hit, k, listing[i])
                    found[i] = jnp.where(hit, offset, found[i])
            for i, entry in enumerate(entries):
                s["tab"][entry + b] = listing[i]
        for i, entry in enumerate(entries):
            s["tab"][entry + 2] = found[i]

    def fill_y(r, carry):
        holders = [g * dp_size + ((x + h) % nx) * ny + y for h in range(nx)]
        fill(g * dp_size + x * ny + (y + r) % ny, holders, [entry_y(h, r) for h in range(nx)])
        return carry

    def fill_z(r, carry):
        own = jnp.where(r == 0, -1000, g * dp_size + dp)
        other = (z * CORES + (1 - c)) * dp_size + dp
        fill((((z + r) % nz) * CORES + c) * dp_size + dp, [own, other], [entry_z(h, r) for h in range(CORES)])
        return carry

    s["qy"][0] = q_ref[...].reshape(lanes, width)
    s["qz"][0] = q_ref[...].reshape(lanes, width)
    lax.fori_loop(0, nz, fill_z, 0)
    lax.fori_loop(0, ny, fill_y, 0)

    lane = lax.broadcasted_iota(jnp.int32, (1, lanes), 1)

    def listing_row(entry):
        row = jnp.full((1, lanes), s["tab"][entry], jnp.int32)
        for b in range(1, qb):
            row = jnp.where(lane >= b * rows, s["tab"][entry + b], row)
        return row

    def score(held, entry, q, index, m_ref, lse_ref, h, r):
        block = held[s["tab"][entry + 2]]
        scores = lax.dot_general(block, q, (((1,), (1,)), ((), ())), preferred_element_type=jnp.float32) * scale
        scores = jnp.where(listing_row(entry) >= 0, scores, NEG)
        top = jnp.max(scores, axis=0, keepdims=True)
        powers = jnp.exp(scores - top)
        s["e"][index] = powers
        m_ref[h, pl.ds(r, 1), :] = top
        lse_ref[h, pl.ds(r, 1), :] = top + jnp.log(jnp.sum(powers, axis=0, keepdims=True))

    def score_y(h, r):
        score(passages[h], entry_y(h, r), s["qy"][r], h * ny + r, s["my"], s["sy"], h, r)

    held_z = [p_ref, s["pc"]]

    def score_z(h, r):
        score(held_z[h], entry_z(h, r), s["qz"][r], nx * ny + h * nz + r, s["mz"], s["sz"], h, r)

    def each(count, first_slot, n, body):
        def step(i, carry):
            body((i + first_slot) % n)
            return carry

        lax.fori_loop(0, count, step, 0)

    def pass_on(t):
        for part in range(qb):
            for n, copy in ((ny, y_copy), (nz, z_copy)):
                if n > 1 and 1 <= t <= n // 2 - 1:
                    for way, piece in line_steps(n, qb, t - 1):
                        if piece == part:
                            copy(way, t - 1, part).wait_recv()
                            if (way, part) in line_steps(n, qb, t):
                                start(copy(way, t, part))

    half_y, half_z, half_x = ny // 2, nz // 2, nx // 2
    pass_on(1)
    pass_on(2)
    for t in range(1, half_x):
        for way, part in sorted(line_steps(nx, owned, t - 1), key=lambda e: (e[1] + (owned // 2 if e[0] else 0)) % owned):
            if (way, part) in line_steps(nx, owned, t):
                x_copy(way, t - 1, part).wait_recv()
                start(x_copy(way, t, part))
    core_gather.wait_recv()
    near_y, near_z = max(half_y - 2, 0), max(half_z - 2, 0)

    def near_pairs_y(r):
        score_y(0, r)

    def pairs_z(r):
        for h in range(CORES):
            score_z(h, r)

    each(2 * near_y + 1, ny - near_y, ny, near_pairs_y)
    pass_on(3)
    each(2 * near_z + 1, nz - near_z, nz, pairs_z)
    for n, copy in ((nz, z_copy), (ny, y_copy)):
        if n > 1:
            for way, part in line_steps(n, qb, n // 2 - 1):
                copy(way, n // 2 - 1, part).wait_recv()
    each(nz - 2 * near_z - 1, near_z + 1, nz, pairs_z)

    def merge(parts):
        top = functools.reduce(jnp.maximum, parts)
        return top + jnp.log(sum(jnp.exp(part - top) for part in parts))

    s["zst"][...] = merge([s["sz"][h] for h in range(CORES)])
    stat_z = spread("stat", nz, at_z, s["zst"], s["zsr"], "tz")
    each(ny - 2 * near_y - 1, near_y + 1, ny, near_pairs_y)

    for t in range(half_x):
        for way, part in line_steps(nx, owned, t):
            if t == half_x - 1 or (way, part) not in line_steps(nx, owned, t + 1):
                if t < half_x - 1:
                    x_copy(way, t, part).wait_recv()
    middle = [h for h in range(1, nx) if h != half_x]

    def side_pairs(r):
        for h in middle:
            score_y(h, r)

    if middle:
        each(ny, 0, ny, side_pairs)
    own_z = [s["zst"][0:1, :]]
    for copy in stat_z:
        copy.wait_recv()
    own_z += [s["zsr"][j][nz - j : nz - j + 1, :] for j in range(1, nz)]
    z_row = merge(own_z)
    if nx > 1:
        for way, part in line_steps(nx, owned, half_x - 1):
            x_copy(way, half_x - 1, part).wait_recv()
        each(ny, 0, ny, lambda r: score_y(half_x, r))

    stat = merge([s["sy"][h] for h in range(nx)])
    ring_row = lax.broadcasted_iota(jnp.int32, (ny, lanes), 0)
    stat = jnp.where(ring_row == 0, merge([stat, jnp.broadcast_to(z_row, stat.shape)]), stat)
    s["yst"][...] = stat
    stat_y = spread("stat", ny, at_y, s["yst"], s["ysr"], "ty")
    for copy in aux_y + aux_z:
        copy.wait_recv()
    for copy in stat_y:
        copy.wait_recv()

    def turned(value, places):
        if ny == 8:
            return pltpu.roll(value, places, axis=0)
        return jnp.concatenate([value[ny - places :], value[: ny - places]], axis=0)

    total = merge([stat] + [turned(s["ysr"][j], j) for j in range(1, ny)])
    s["ya"][...] = total
    s["fin"][...] = jnp.broadcast_to(total[0:1, :], (8, lanes))
    fin_z = spread("fin", nz, at_z, s["fin"], s["zfr"], "fz")

    down = lax.broadcasted_iota(jnp.int32, (rows, lanes), 0).astype(jnp.float32)

    def dscore(index, entry, m_row, a_row, w_line, pos_line):
        factor = jnp.exp(m_row - a_row) * w_line
        spot = pos_line - (listing_row(entry) * rows).astype(jnp.float32)
        value = s["e"][index] * factor - jnp.where(down == spot, w_line, 0.0)
        s["d"][index] = value.astype(jnp.bfloat16)

    def dscore_y(h, r):
        dscore(
            h * ny + r,
            entry_y(h, r),
            s["my"][h, pl.ds(r, 1), :],
            s["ya"][pl.ds(r, 1), :],
            s["auxy"][r, 0:1, :],
            s["auxy"][r, 1:2, :],
        )

    def dscore_z(h, r, a_row):
        dscore(
            nx * ny + h * nz + r,
            entry_z(h, r),
            s["mz"][h, pl.ds(r, 1), :],
            a_row,
            s["auxz"][r, 0:1, :],
            s["auxz"][r, 1:2, :],
        )

    def term(index, q, r):
        s["t"][r] = jnp.dot(s["d"][index], q, preferred_element_type=jnp.float32)

    strip = min(rows, 32)

    def collect(out, n, entry):
        def block(i, carry):
            p = i // (rows // strip)
            part = pl.ds((i % (rows // strip)) * strip, strip)
            acc = jnp.zeros((strip, width), jnp.float32)
            for r in range(n):
                acc += jnp.where(s["tab"][entry(r) + 2] == p, 1.0, 0.0) * s["t"][r, part, :]
            out[p, part, :] = acc.astype(out.dtype)
            return carry

        lax.fori_loop(0, owned * (rows // strip), block, 0)

    def terms_y(h, r):
        term(h * ny + r, s["qy"][r], r)

    def query_part(out, r, pairs):
        acc = None
        for index, held, entry in pairs:
            block = held[s["tab"][entry + 2]]
            part = lax.dot_general(
                s["d"][index], block, (((0,), (0,)), ((), ())), preferred_element_type=jnp.float32
            )
            acc = part if acc is None else acc + part
        out[r] = acc

    def reduce_copy(line, n, device_at, way, t, part):
        return send(
            s[line + "o"].at[way, t - 1, part],
            s[line + "i"].at[way, t - 1, part],
            s["r" + line + "_s"].at[way, t - 1, part],
            s["r" + line + "_r"].at[way, t - 1, part],
            device_at(1 if way == 0 else n - 1),
        )

    def reduce_send(line, n, device_at, way, t, part, value, alone):
        if not alone:
            reduce_copy(line, n, device_at, way, t + 1, part).wait_recv()
            value = value + s[line + "i"][way, t, part].astype(jnp.float32)
        s[line + "o"][way, t - 1, part] = value.astype(jnp.bfloat16)
        start(reduce_copy(line, n, device_at, way, t, part))

    def query_send(line, n, device_at, t, alone):
        if t < 1 or t > n // 2:
            return
        for part in range(qb):
            for way in (0, 1):
                if (way, part) not in line_steps(n, qb, t - 1):
                    continue
                first_here = t == n // 2 or (way, part) not in line_steps(n, qb, t)
                if first_here != alone:
                    continue
                target = t if way == 0 else (n - t) % n
                value = s["gq" + line][target, pl.ds(part * rows, rows), :]
                reduce_send(line, n, device_at, way, t, part, value, alone)

    def passage_send(t, alone):
        for part in range(owned):
            for way in (0, 1):
                if (way, part) not in line_steps(nx, owned, t - 1):
                    continue
                first_here = t == half_x or (way, part) not in line_steps(nx, owned, t)
                if first_here != alone:
                    continue
                target = t if way == 0 else (nx - t) % nx
                reduce_send("x", nx, at_x, way, t, part, s["gp"][target, part], alone)

    def grad_x(h):
        def both(r):
            terms_y(h, r)

        each(ny, 0, ny, both)
        collect(s["gp"].at[h], ny, lambda r: entry_y(h, r))

    if nx > 1:
        each(ny, 0, ny, lambda r: dscore_y(half_x, r))
        grad_x(half_x)
        passage_send(half_x, True)
    rest = [h for h in range(nx) if nx == 1 or h != half_x]

    def query_y(r):
        for h in rest:
            dscore_y(h, r)
        query_part(s["gqy"], r, [(h * ny + r, passages[h], entry_y(h, r)) for h in range(nx)])

    far_y = min(3, ny)
    start_y = (half_y - 1) % ny
    each(far_y, start_y, ny, query_y)
    query_send("y", ny, at_y, half_y, True)
    query_send("y", ny, at_y, half_y - 1, True)
    each(ny - far_y, (start_y + far_y) % ny, ny, query_y)
    for t in range(half_x - 1, 0, -1):
        for h in sorted({t, nx - t}):
            grad_x(h)
        passage_send(t, True)
    if half_y > 1:
        query_send("y", ny, at_y, half_y - 1, False)

    for copy in fin_z:
        copy.wait_recv()
    s["zfr"][0] = s["fin"][...]

    def query_z(r):
        a_row = s["zfr"][r, 0:1, :]
        for h in range(CORES):
            dscore_z(h, r, a_row)
        query_part(s["gqz"], r, [(nx * ny + h * nz + r, held_z[h], entry_z(h, r)) for h in range(CORES)])

    far_z = min(3, nz)
    start_z = (half_z - 1) % nz
    each(far_z, start_z, nz, query_z)
    query_send("z", nz, at_z, half_z, True)
    query_send("z", nz, at_z, half_z - 1, True)
    each(nz - far_z, (start_z + far_z) % nz, nz, query_z)
    query_send("y", ny, at_y, half_y - 2, False) if half_y > 2 else None
    if half_z > 1:
        query_send("z", nz, at_z, half_z - 1, False)

    def grad_z(h):
        each(nz, 0, nz, lambda r: term(nx * ny + h * nz + r, s["qz"][r], r))
        out = s["co"] if h == 1 else s["gp"].at[nx]
        collect(out, nz, lambda r: entry_z(h, r))

    grad_z(1)
    core_reduce = send(s["co"], s["ci"], s["cs"].at[2], s["cs"].at[3], partner)
    start(core_reduce)
    for t in range(half_x - 1, 0, -1):
        passage_send(t, False)
    for t in range(half_y - 3, 0, -1):
        query_send("y", ny, at_y, t, False)
    grad_z(0)
    grad_x(0)
    for t in range(half_z - 2, 0, -1):
        query_send("z", nz, at_z, t, False)

    def arrived(line, n, device_at, parts, part):
        total = None
        for way in (0, 1):
            if n > 1 and (way, part) in line_steps(n, parts, 0):
                reduce_copy(line, n, device_at, way, 1, part).wait_recv()
                value = s[line + "i"][way, 0, part].astype(jnp.float32)
                total = value if total is None else total + value
        return 0.0 if total is None else total

    for part in range(qb):
        block = pl.ds(part * rows, rows)
        value = s["gqy"][0, block, :] + s["gqz"][0, block, :]
        value += arrived("y", ny, at_y, qb, part)
        value += arrived("z", nz, at_z, qb, part)
        gq_ref[part] = value.astype(gq_ref.dtype)
    core_reduce.wait_recv()
    for part in range(owned):
        value = s["gp"][0, part] + s["gp"][nx, part] + s["ci"][part].astype(jnp.float32)
        value += arrived("x", nx, at_x, owned, part)
        gp_ref[part] = value.astype(gp_ref.dtype)
    for copy in started:
        copy.wait_send()


def solution(mesh, sizes=SIZES):
    nx, ny = sizes
    nz = mesh.shape["group"] // CORES
    assert mesh.shape["dp"] == nx * ny

    def shards(queries, passages, candidates, positives, row_weight, owner_map):
        plan = scratch_plan(nx, ny, nz, queries.shape[0], *passages.shape)
        vmem = pl.BlockSpec(memory_space=pltpu.VMEM)
        smem = pl.BlockSpec(memory_space=pltpu.SMEM)
        return pl.pallas_call(
            functools.partial(kernel, (nx, ny, nz), tuple(plan)),
            out_shape=(
                jax.ShapeDtypeStruct(queries.shape, queries.dtype),
                jax.ShapeDtypeStruct(passages.shape, passages.dtype),
            ),
            in_specs=[vmem, vmem, smem, smem, vmem, vmem],
            out_specs=(vmem, vmem),
            scratch_shapes=list(plan.values()),
            compiler_params=pltpu.CompilerParams(
                collective_id=0, has_side_effects=True, vmem_limit_bytes=64_000_000
            ),
        )(queries, passages, candidates.T, owner_map, positives, row_weight)

    return jax.shard_map(
        shards,
        mesh=mesh,
        in_specs=(
            P(("group", "dp"), None, None),
            P(("group", "dp"), None, None),
            P(),
            P(("group", "dp"), None),
            P(("group", "dp"), None),
            P(),
        ),
        out_specs=(P(("group", "dp"), None, None), P(("group", "dp"), None, None)),
        check_vma=False,
    )
```

```python
import functools
import math

import jax
import jax.numpy as jnp
from jax import lax
from jax.experimental import pallas as pl
from jax.experimental.pallas import tpu as pltpu
from jax.sharding import PartitionSpec as P

MESH = pl.DeviceIdType.MESH
NEG = -1e30
CORES = 2
SIZES = (4, 8)


def scratch_plan(nx, ny, nz, qb, owned, rows, width, cand_shape, map_shape):
    lanes = qb * rows
    dma = pltpu.SemaphoreType.DMA
    bf, f32 = jnp.bfloat16, jnp.float32
    plan = {
        "qy": pltpu.VMEM((ny, lanes, width), bf),
        "qz": pltpu.VMEM((nz, lanes, width), bf),
        "pc": pltpu.VMEM((owned, rows, width), bf),
        "tab": pltpu.SMEM(((nx * ny + CORES * nz) * 3,), jnp.int32),
        "auxy": pltpu.VMEM((ny, 8, lanes), f32),
        "auxz": pltpu.VMEM((nz, 8, lanes), f32),
        "e": pltpu.VMEM((nx * ny + CORES * nz, rows, lanes), f32),
        "d": pltpu.VMEM((nx * ny + CORES * nz, rows, lanes), bf),
        "my": pltpu.VMEM((nx, ny, lanes), f32),
        "sy": pltpu.VMEM((nx, ny, lanes), f32),
        "mz": pltpu.VMEM((CORES, nz, lanes), f32),
        "sz": pltpu.VMEM((CORES, nz, lanes), f32),
        "zst": pltpu.VMEM((nz, lanes), f32),
        "zsr": pltpu.VMEM((nz, nz, lanes), f32),
        "yst": pltpu.VMEM((ny, lanes), f32),
        "ysr": pltpu.VMEM((ny, ny, lanes), f32),
        "ya": pltpu.VMEM((ny, lanes), f32),
        "fin": pltpu.VMEM((8, lanes), f32),
        "zfr": pltpu.VMEM((nz, 8, lanes), f32),
        "gqy": pltpu.VMEM((ny, lanes, width), f32),
        "gqz": pltpu.VMEM((nz, lanes, width), f32),
        "chain": pltpu.VMEM((nx + CORES, max(ny, nz) + 1, rows, width), f32),
        "own": pltpu.VMEM((owned, rows, width), f32),
        "yo": pltpu.VMEM((max(ny - 1, 1) * qb, rows, width), bf),
        "yi": pltpu.VMEM((max(ny - 1, 1) * qb, rows, width), bf),
        "zo": pltpu.VMEM((max(nz - 1, 1) * qb, rows, width), bf),
        "zi": pltpu.VMEM((max(nz - 1, 1) * qb, rows, width), bf),
        "xo": pltpu.VMEM((max(nx - 1, 1) * owned, rows, width), bf),
        "xi": pltpu.VMEM((max(nx - 1, 1) * owned, rows, width), bf),
        "co": pltpu.VMEM((owned, rows, width), bf),
        "ci": pltpu.VMEM((owned, rows, width), bf),
        "gqo": pltpu.VMEM((qb, rows, width), bf),
        "gpo": pltpu.VMEM((owned, rows, width), bf),
        "p0": pltpu.VMEM((owned, rows, width), bf),
        "cand": pltpu.SMEM(cand_shape, jnp.int32),
        "map": pltpu.SMEM(map_shape, jnp.int32),
        "posv": pltpu.VMEM((qb, rows), jnp.int32),
        "wv": pltpu.VMEM((qb, rows), f32),
        "links": pltpu.SMEM(((nx + CORES) * (max(ny, nz) + owned),), jnp.int32),
        "sent": dma((13,)),
        "got": dma((8,)),
        "near": dma((7,)),
        "yr": dma((max(ny - 1, 1) * qb,)),
        "zr": dma((max(nz - 1, 1) * qb,)),
        "xr": dma((max(nx - 1, 1) * owned,)),
        "xr2": dma((max(nx - 1, 1) * owned,)),
    }
    for h in range(1, nx):
        plan[f"px{h}"] = pltpu.VMEM((owned, rows, width), bf)
    return plan


def kernel(sizes, names, q_ref, p_ref, cand_ref, own_ref, pos_ref, w_ref, gq_ref, gp_ref, *scratch):
    nx, ny, nz = sizes
    s = dict(zip(names, scratch))
    qb, rows, width = q_ref.shape
    owned = p_ref.shape[0]
    ncand = cand_ref.shape[0]
    lanes = qb * rows
    scale = 3.0 / math.sqrt(width)
    dp_size = nx * ny
    g, dp = lax.axis_index("group"), lax.axis_index("dp")
    x, y = dp // ny, dp % ny
    z, c = g // CORES, g % CORES

    def at_y(r):
        return (g, x * ny + (y + r) % ny)

    def at_x(r):
        return (g, ((x + r) % nx) * ny + y)

    def at_z(r):
        return (((z + r) % nz) * CORES + c, dp)

    partner = (z * CORES + (1 - c), dp)

    peers = [at_y(r) for r in range(1, ny)] + [at_z(r) for r in range(1, nz)] + [partner]
    peers += [at_x(r) for r in sorted({1 % nx, (nx - 1) % nx} - {0})]
    def fetch(src, dst, sem):
        copy = pltpu.make_async_copy(src, dst, s["near"].at[sem])
        copy.start()
        return copy

    scalars = [fetch(cand_ref, s["cand"], 0), fetch(own_ref, s["map"], 1)]
    rows_in = [fetch(pos_ref, s["posv"], 2), fetch(w_ref, s["wv"], 3)]
    barrier = pltpu.get_barrier_semaphore()
    for peer in peers:
        pl.semaphore_signal(barrier, inc=1, device_id=peer, device_id_type=MESH)
    pl.semaphore_wait(barrier, len(peers))

    def send(src, dst, family, recv_sem, device):
        return pltpu.make_async_remote_copy(
            src_ref=src,
            dst_ref=dst,
            send_sem=s["sent"].at[family],
            recv_sem=recv_sem,
            device_id=device,
            device_id_type=MESH,
        )

    def start(copy):
        copy.start()

    def all_sent(family, extent):
        send(extent, extent, family, s["got"].at[7], partner).wait_send()

    def line_steps(n, parts, t):
        half = n // 2
        if t < half - 1:
            return [(way, part) for part in range(parts) for way in (0, 1)]
        return [(way, part) for part in range(parts) for way in (0, 1) if (part >= parts // 2) == (way == 1)]

    def slots(n, way, t):
        return ((-t) % n, (-(t + 1)) % n) if way == 0 else (t, t + 1)

    def entry(n, parts, way, t, part):
        half = n // 2
        return (2 * t + way) * parts + part if t < half - 1 else 2 * (half - 1) * parts + part

    def query_copy(line, n, device_at, way, t, part):
        src, dst = slots(n, way, t)
        buf = s["q" + line]
        block = pl.ds(part * rows, rows)
        return send(
            q_ref.at[part] if t == 0 else buf.at[src, block],
            buf.at[dst, block],
            "yz".index(line),
            s[line + "r"].at[entry(n, qb, way, t, part)],
            device_at(1 if way == 0 else n - 1),
        )

    def y_copy(way, t, part):
        return query_copy("y", ny, at_y, way, t, part)

    def z_copy(way, t, part):
        return query_copy("z", nz, at_z, way, t, part)

    passages = [s["p0"]] + [s[f"px{h}"] for h in range(1, nx)]

    def x_copy(way, t, part):
        src, dst = slots(nx, way, t)
        return send(
            p_ref.at[part] if t == 0 else passages[src].at[part],
            passages[dst].at[part],
            2,
            s["xr"].at[entry(nx, owned, way, t, part)],
            at_x(1 if way == 0 else nx - 1),
        )

    if ny > 1:
        for way, part in line_steps(ny, qb, 0):
            start(y_copy(way, 0, part))
    if nz > 1:
        for way, part in line_steps(nz, qb, 0):
            start(z_copy(way, 0, part))
    first = sorted(line_steps(nx, owned, 0), key=lambda e: (e[1] + (owned // 2 if e[0] else 0)) % owned)
    for way, part in first:
        start(x_copy(way, 0, part))
    core_gather = send(p_ref, s["pc"], 3, s["got"].at[0], partner)
    start(core_gather)

    whole_q = [fetch(q_ref.at[b], s["qy"].at[0, pl.ds(b * rows, rows)], 4 + b) for b in range(qb)]
    whole_p = fetch(p_ref, s["p0"], 4 + qb)
    for copy in rows_in:
        copy.wait()
    tile_row = lax.broadcasted_iota(jnp.int32, (8, lanes), 0)
    w_row = jnp.concatenate([s["wv"][b : b + 1, :] for b in range(qb)], axis=1) * scale
    pos_row = jnp.concatenate([s["posv"][b : b + 1, :] for b in range(qb)], axis=1).astype(jnp.float32)
    own_aux = jnp.where(tile_row == 0, w_row, jnp.where(tile_row == 1, pos_row, 0.0))
    s["auxy"][0] = own_aux
    s["auxz"][0] = own_aux

    def spread(n, device_at, src, dst, family):
        for r in range(1, n):
            start(send(src, dst.at[n - r], family, s["got"].at[family - 3], device_at(r)))

        def wait():
            if n > 1:
                extent = dst.at[pl.ds(1, n - 1)]
                send(extent, extent, family, s["got"].at[family - 3], partner).wait_recv()

        return wait

    def entry_y(h, r):
        return (h * ny + r) * 3

    def entry_z(h, r):
        return (nx * ny + h * nz + r) * 3

    def fill(lister, holders, entries):
        found = [jnp.int32(0)] * len(holders)
        for b in range(qb):
            listing = [jnp.int32(-1)] * len(holders)
            for k in range(ncand):
                place = s["map"][s["cand"][k, lister * qb + b]]
                for i, holder in enumerate(holders):
                    offset = place - holder * owned
                    hit = (offset >= 0) & (offset < owned)
                    listing[i] = jnp.where(hit, k, listing[i])
                    found[i] = jnp.where(hit, offset, found[i])
            for i, entry in enumerate(entries):
                s["tab"][entry + b] = listing[i]
        for i, entry in enumerate(entries):
            s["tab"][entry + 2] = found[i]

    def fill_y(r, carry):
        holders = [g * dp_size + ((x + h) % nx) * ny + y for h in range(nx)]
        fill(g * dp_size + x * ny + (y + r) % ny, holders, [entry_y(h, r) for h in range(nx)])
        return carry

    def fill_z(r, carry):
        own = jnp.where(r == 0, -1000, g * dp_size + dp)
        other = (z * CORES + (1 - c)) * dp_size + dp
        fill((((z + r) % nz) * CORES + c) * dp_size + dp, [own, other], [entry_z(h, r) for h in range(CORES)])
        return carry

    for copy in scalars:
        copy.wait()
    lax.fori_loop(0, nz, fill_z, 0)
    for copy in whole_q:
        copy.wait()
    s["qz"][0] = s["qy"][0]
    whole_p.wait()
    aux_y = spread(ny, at_y, s["auxy"].at[0], s["auxy"], 4)
    aux_z = spread(nz, at_z, s["auxz"].at[0], s["auxz"], 5)

    lane = lax.broadcasted_iota(jnp.int32, (1, lanes), 1)

    def listing_row(entry):
        row = jnp.full((1, lanes), s["tab"][entry], jnp.int32)
        for b in range(1, qb):
            row = jnp.where(lane >= b * rows, s["tab"][entry + b], row)
        return row

    def score(pairs, q):
        blocks = [held[s["tab"][where + 2]] for held, where, _, _, _ in pairs]
        block = jnp.concatenate(blocks, axis=0) if len(blocks) > 1 else blocks[0]
        joined = lax.dot_general(block, q, (((1,), (1,)), ((), ())), preferred_element_type=jnp.float32) * scale
        for i, (_, where, index, (top_ref, lse_ref, h), r) in enumerate(pairs):
            scores = joined[i * rows : (i + 1) * rows]
            scores = jnp.where(listing_row(where) >= 0, scores, NEG)
            top = jnp.max(scores, axis=0, keepdims=True)
            powers = jnp.exp(scores - top)
            s["e"][index] = powers
            top_ref[h, pl.ds(r, 1), :] = top
            lse_ref[h, pl.ds(r, 1), :] = top + jnp.log(jnp.sum(powers, axis=0, keepdims=True))

    def score_y(hs, r):
        score([(passages[h], entry_y(h, r), h * ny + r, (s["my"], s["sy"], h), r) for h in hs], s["qy"][r])

    held_z = [s["p0"], s["pc"]]

    def score_z(r):
        pairs = [(held_z[h], entry_z(h, r), nx * ny + h * nz + r, (s["mz"], s["sz"], h), r) for h in range(CORES)]
        score(pairs, s["qz"][r])

    def each(count, first_slot, n, body):
        def step(i, carry):
            body((i + first_slot) % n)
            return carry

        lax.fori_loop(0, count, step, 0)

    def pass_on(t):
        for part in range(qb):
            for n, copy in ((ny, y_copy), (nz, z_copy)):
                if n > 1 and 1 <= t <= n // 2 - 1:
                    for way, piece in line_steps(n, qb, t - 1):
                        if piece == part:
                            copy(way, t - 1, part).wait_recv()
                            if (way, part) in line_steps(n, qb, t):
                                start(copy(way, t, part))

    half_y, half_z, half_x = ny // 2, nz // 2, nx // 2
    pass_on(1)
    lax.fori_loop(0, ny, fill_y, 0)
    pass_on(2)
    for t in range(1, half_x):
        for way, part in sorted(line_steps(nx, owned, t - 1), key=lambda e: (e[1] + (owned // 2 if e[0] else 0)) % owned):
            if (way, part) in line_steps(nx, owned, t):
                x_copy(way, t - 1, part).wait_recv()
                start(x_copy(way, t, part))
    core_gather.wait_recv()
    near_y, near_z = max(half_y - 2, 0), max(half_z - 2, 0)

    def near_pairs_y(r):
        score_y([0], r)

    span = max(ny, nz) + owned
    for h in range(nx + CORES):
        n = ny if h < nx else nz
        found = [s["tab"][(entry_y(h, r) if h < nx else entry_z(h - nx, r)) + 2] for r in range(n)]
        for r in range(n):
            before = jnp.int32(0)
            for other in range(r):
                before = jnp.where(found[other] == found[r], other + 1, before)
            s["links"][h * span + r] = before
        for p in range(owned):
            last = jnp.int32(0)
            for r in range(n):
                last = jnp.where(found[r] == p, r + 1, last)
            s["links"][h * span + max(ny, nz) + p] = last
        s["chain"][h, 0] = jnp.zeros((rows, width), jnp.float32)

    each(2 * near_y + 1, ny - near_y, ny, near_pairs_y)
    pass_on(3)
    each(2 * near_z + 1, nz - near_z, nz, score_z)
    for n, copy in ((nz, z_copy), (ny, y_copy)):
        if n > 1:
            for way, part in line_steps(n, qb, n // 2 - 1):
                copy(way, n // 2 - 1, part).wait_recv()
    each(nz - 2 * near_z - 1, near_z + 1, nz, score_z)

    def merge(parts):
        top = functools.reduce(jnp.maximum, parts)
        return top + jnp.log(sum(jnp.exp(part - top) for part in parts))

    s["zst"][...] = merge([s["sz"][h] for h in range(CORES)])
    stat_z = spread(nz, at_z, s["zst"], s["zsr"], 6)
    each(ny - 2 * near_y - 1, near_y + 1, ny, near_pairs_y)

    for t in range(half_x):
        for way, part in line_steps(nx, owned, t):
            if t == half_x - 1 or (way, part) not in line_steps(nx, owned, t + 1):
                if t < half_x - 1:
                    x_copy(way, t, part).wait_recv()
    middle = [h for h in range(1, nx) if h != half_x]

    if middle:
        each(ny, 0, ny, lambda r: score_y(middle, r))
    own_z = [s["zst"][0:1, :]]
    stat_z()
    own_z += [s["zsr"][j][nz - j : nz - j + 1, :] for j in range(1, nz)]
    z_row = merge(own_z)
    if nx > 1:
        for way, part in line_steps(nx, owned, half_x - 1):
            x_copy(way, half_x - 1, part).wait_recv()

        def last_pairs(i):
            score_y([half_x], i)
            score_y([half_x], i + ny // 2)

        each(ny // 2, 0, ny, last_pairs)

    stat = merge([s["sy"][h] for h in range(nx)])
    ring_row = lax.broadcasted_iota(jnp.int32, (ny, lanes), 0)
    stat = jnp.where(ring_row == 0, merge([stat, jnp.broadcast_to(z_row, stat.shape)]), stat)
    s["yst"][...] = stat
    stat_y = spread(ny, at_y, s["yst"], s["ysr"], 7)
    aux_y()
    aux_z()
    stat_y()

    def turned(value, places):
        if ny == 8:
            return pltpu.roll(value, places, axis=0)
        return jnp.concatenate([value[ny - places :], value[: ny - places]], axis=0)

    total = merge([stat] + [turned(s["ysr"][j], j) for j in range(1, ny)])
    s["ya"][...] = total
    s["fin"][...] = jnp.broadcast_to(total[0:1, :], (8, lanes))
    fin_z = spread(nz, at_z, s["fin"], s["zfr"], 8)

    down = lax.broadcasted_iota(jnp.int32, (rows, lanes), 0).astype(jnp.float32)

    def dscore(index, entry, m_row, a_row, w_line, pos_line):
        factor = jnp.exp(m_row - a_row) * w_line
        spot = pos_line - (listing_row(entry) * rows).astype(jnp.float32)
        value = s["e"][index] * factor - jnp.where(down == spot, w_line, 0.0)
        s["d"][index] = value.astype(jnp.bfloat16)

    def dscore_y(h, r):
        dscore(
            h * ny + r,
            entry_y(h, r),
            s["my"][h, pl.ds(r, 1), :],
            s["ya"][pl.ds(r, 1), :],
            s["auxy"][r, 0:1, :],
            s["auxy"][r, 1:2, :],
        )

    def dscore_z(h, r, a_row):
        dscore(
            nx * ny + h * nz + r,
            entry_z(h, r),
            s["mz"][h, pl.ds(r, 1), :],
            a_row,
            s["auxz"][r, 0:1, :],
            s["auxz"][r, 1:2, :],
        )

    def term(h, r, index, q):
        value = jnp.dot(s["d"][index], q, preferred_element_type=jnp.float32)
        s["chain"][h, r + 1] = value + s["chain"][h, s["links"][h * span + r]]

    def block_sum(h, p):
        return s["chain"][h, s["links"][h * span + max(ny, nz) + p]]

    def query_part(out, r, pairs):
        left = jnp.concatenate([s["d"][index] for index, _, _ in pairs], axis=0)
        right = jnp.concatenate([held[s["tab"][where + 2]] for _, held, where in pairs], axis=0)
        out[r] = lax.dot_general(left, right, (((0,), (0,)), ((), ())), preferred_element_type=jnp.float32)

    def reduce_copy(line, n, device_at, way, t, part):
        place = entry(n, owned if line == "x" else qb, way, t - 1, part)
        return send(
            s[line + "o"].at[place],
            s[line + "i"].at[place],
            9 + "yzx".index(line),
            s["xr2" if line == "x" else line + "r"].at[place],
            device_at(1 if way == 0 else n - 1),
        )

    def came(line, n, way, t, part):
        return s[line + "i"][entry(n, owned if line == "x" else qb, way, t - 1, part)].astype(jnp.float32)

    def reduce_send(line, n, device_at, way, t, part, value, alone):
        if not alone:
            reduce_copy(line, n, device_at, way, t + 1, part).wait_recv()
            value = value + came(line, n, way, t + 1, part)
        s[line + "o"][entry(n, owned if line == "x" else qb, way, t - 1, part)] = value.astype(jnp.bfloat16)
        start(reduce_copy(line, n, device_at, way, t, part))

    def query_send(line, n, device_at, t, alone):
        if t < 1 or t > n // 2:
            return
        for part in range(qb):
            for way in (0, 1):
                if (way, part) not in line_steps(n, qb, t - 1):
                    continue
                first_here = t == n // 2 or (way, part) not in line_steps(n, qb, t)
                if first_here != alone:
                    continue
                target = t if way == 0 else (n - t) % n
                value = s["gq" + line][target, pl.ds(part * rows, rows), :]
                reduce_send(line, n, device_at, way, t, part, value, alone)

    def passage_send(t, alone):
        for part in range(owned):
            for way in (0, 1):
                if (way, part) not in line_steps(nx, owned, t - 1):
                    continue
                first_here = t == half_x or (way, part) not in line_steps(nx, owned, t)
                if first_here != alone:
                    continue
                target = t if way == 0 else (nx - t) % nx
                reduce_send("x", nx, at_x, way, t, part, block_sum(target, part), alone)

    def grad_x(h):
        each(ny, 0, ny, lambda r: term(h, r, h * ny + r, s["qy"][r]))

    if nx > 1:

        def first_terms(r):
            dscore_y(half_x, r)
            term(half_x, r, half_x * ny + r, s["qy"][r])

        each(ny, 0, ny, first_terms)
        passage_send(half_x, True)
    rest = [h for h in range(nx) if nx == 1 or h != half_x]

    def query_y(r):
        for h in rest:
            dscore_y(h, r)
        query_part(s["gqy"], r, [(h * ny + r, passages[h], entry_y(h, r)) for h in range(nx)])

    far_y = min(3, ny)
    start_y = (half_y - 1) % ny
    each(far_y, start_y, ny, query_y)
    query_send("y", ny, at_y, half_y, True)
    query_send("y", ny, at_y, half_y - 1, True)
    each(ny - far_y, (start_y + far_y) % ny, ny, query_y)
    for t in range(half_x - 1, 0, -1):
        for h in sorted({t, nx - t}):
            grad_x(h)
        passage_send(t, True)
    if half_y > 1:
        query_send("y", ny, at_y, half_y - 1, False)
    fin_z()
    s["zfr"][0] = s["fin"][...]

    def query_z(r):
        a_row = s["zfr"][r, 0:1, :]
        for h in range(CORES):
            dscore_z(h, r, a_row)
        query_part(s["gqz"], r, [(nx * ny + h * nz + r, held_z[h], entry_z(h, r)) for h in range(CORES)])

    far_z = min(3, nz)
    start_z = (half_z - 1) % nz
    each(far_z, start_z, nz, query_z)
    query_send("z", nz, at_z, half_z, True)
    query_send("z", nz, at_z, half_z - 1, True)
    each(nz - far_z, (start_z + far_z) % nz, nz, query_z)
    query_send("y", ny, at_y, half_y - 2, False) if half_y > 2 else None
    if half_z > 1:
        query_send("z", nz, at_z, half_z - 1, False)

    def grad_z(h):
        each(nz, 0, nz, lambda r: term(nx + h, r, nx * ny + h * nz + r, s["qz"][r]))

    for t in range(half_x - 1, 0, -1):
        passage_send(t, False)
    grad_z(1)
    for part in range(owned):
        s["co"][part] = block_sum(nx + 1, part).astype(jnp.bfloat16)
    core_reduce = send(s["co"], s["ci"], 12, s["got"].at[6], partner)
    start(core_reduce)
    for t in range(half_y - 3, 0, -1):
        query_send("y", ny, at_y, t, False)
    grad_z(0)
    grad_x(0)
    for t in range(half_z - 2, 0, -1):
        query_send("z", nz, at_z, t, False)

    def arrived(line, n, device_at, parts, part):
        total = None
        for way in (0, 1):
            if n > 1 and (way, part) in line_steps(n, parts, 0):
                reduce_copy(line, n, device_at, way, 1, part).wait_recv()
                value = came(line, n, way, 1, part)
                total = value if total is None else total + value
        return 0.0 if total is None else total

    core_reduce.wait_recv()
    for part in range(owned):
        s["own"][part] = block_sum(0, part) + block_sum(nx, part) + s["ci"][part].astype(jnp.float32)
    results = []
    for part in range(qb):
        block = pl.ds(part * rows, rows)
        value = s["gqy"][0, block, :] + s["gqz"][0, block, :]
        value += arrived("y", ny, at_y, qb, part)
        value += arrived("z", nz, at_z, qb, part)
        s["gqo"][part] = value.astype(gq_ref.dtype)
    results.append(fetch(s["gqo"], gq_ref, 0))
    for part in range(owned):
        value = s["own"][part] + arrived("x", nx, at_x, owned, part)
        s["gpo"][part] = value.astype(gp_ref.dtype)
    results.append(fetch(s["gpo"], gp_ref, 1))
    if ny > 1:
        for family, extent in ((0, s["yo"]), (9, s["yo"]), (4, s["auxy"].at[pl.ds(1, ny - 1)]), (7, s["ysr"].at[pl.ds(1, ny - 1)])):
            all_sent(family, extent)
    if nz > 1:
        for family, extent in ((1, s["zo"]), (10, s["zo"]), (5, s["auxz"].at[pl.ds(1, nz - 1)])):
            all_sent(family, extent)
        for family, extent in ((6, s["zsr"].at[pl.ds(1, nz - 1)]), (8, s["zfr"].at[pl.ds(1, nz - 1)])):
            all_sent(family, extent)
    if nx > 1:
        all_sent(2, s["xo"])
        all_sent(11, s["xo"])
    all_sent(3, s["pc"])
    all_sent(12, s["co"])
    for copy in results:
        copy.wait()


def hand_over(gq_in, gp_in, gq_out, gp_out, gq, gp, sems):
    pieces = [(gq_in, gq, gq_out, 0)] + [(gp_in, gp, gp_out, part) for part in range(gp_in.shape[0])]
    loads, stores = [], []
    for i, (src, held, dst, part) in enumerate(pieces):
        piece = slice(None) if i == 0 else pl.ds(part, 1)
        loads.append(pltpu.make_async_copy(src.at[piece], held.at[piece], sems.at[0, i]))
        stores.append(pltpu.make_async_copy(held.at[piece], dst.at[piece], sems.at[1, i]))
    for load in loads:
        load.start()
    for load, store in zip(loads, stores):
        load.wait()
        store.start()
    for store in stores:
        store.wait()


def solution(mesh, sizes=SIZES):
    nx, ny = sizes
    nz = mesh.shape["group"] // CORES
    assert mesh.shape["dp"] == nx * ny

    def shards(queries, passages, candidates, positives, row_weight, owner_map):
        listed = candidates.T
        plan = scratch_plan(nx, ny, nz, queries.shape[0], *passages.shape, listed.shape, owner_map.shape)
        left = pl.BlockSpec(memory_space=pl.ANY)
        shapes = (
            jax.ShapeDtypeStruct(queries.shape, queries.dtype),
            jax.ShapeDtypeStruct(passages.shape, passages.dtype),
        )
        results = pl.pallas_call(
            functools.partial(kernel, (nx, ny, nz), tuple(plan)),
            out_shape=shapes,
            in_specs=[left] * 6,
            out_specs=(left, left),
            scratch_shapes=list(plan.values()),
            compiler_params=pltpu.CompilerParams(
                collective_id=0, has_side_effects=True, vmem_limit_bytes=64_000_000
            ),
        )(queries, passages, listed, owner_map, positives, row_weight)
        return pl.pallas_call(
            hand_over,
            out_shape=shapes,
            in_specs=[left] * 2,
            out_specs=(left, left),
            scratch_shapes=[
                pltpu.VMEM(queries.shape, queries.dtype),
                pltpu.VMEM(passages.shape, passages.dtype),
                pltpu.SemaphoreType.DMA((2, passages.shape[0] + 1)),
            ],
        )(*results)

    return jax.shard_map(
        shards,
        mesh=mesh,
        in_specs=(
            P(("group", "dp"), None, None),
            P(("group", "dp"), None, None),
            P(),
            P(("group", "dp"), None),
            P(("group", "dp"), None),
            P(),
        ),
        out_specs=(P(("group", "dp"), None, None), P(("group", "dp"), None, None)),
        check_vma=False,
    )
```

```python
import functools
import math

import jax
import jax.numpy as jnp
from jax import lax
from jax.experimental import pallas as pl
from jax.experimental.pallas import tpu as pltpu
from jax.sharding import PartitionSpec as P

MESH = pl.DeviceIdType.MESH
NEG = -1e30
CORES = 2
SIZES = (4, 8)


def scratch_plan(nx, ny, nz, qb, owned, rows, width, cand_shape, map_shape):
    lanes = qb * rows
    dma = pltpu.SemaphoreType.DMA
    bf, f32 = jnp.bfloat16, jnp.float32
    plan = {
        "qy": pltpu.VMEM((ny, lanes, width), bf),
        "qz": pltpu.VMEM((nz, lanes, width), bf),
        "pc": pltpu.VMEM((owned, rows, width), bf),
        "tab": pltpu.SMEM(((nx * ny + CORES * nz) * 3,), jnp.int32),
        "auxy": pltpu.VMEM((ny, 8, lanes), f32),
        "auxz": pltpu.VMEM((nz, 8, lanes), f32),
        "e": pltpu.VMEM((nx * ny + CORES * nz, rows, lanes), f32),
        "d": pltpu.VMEM((nx * ny + CORES * nz, rows, lanes), bf),
        "my": pltpu.VMEM((nx, ny, lanes), f32),
        "sy": pltpu.VMEM((nx, ny, lanes), f32),
        "mz": pltpu.VMEM((CORES, nz, lanes), f32),
        "sz": pltpu.VMEM((CORES, nz, lanes), f32),
        "zst": pltpu.VMEM((nz, lanes), f32),
        "zsr": pltpu.VMEM((nz, nz, lanes), f32),
        "yst": pltpu.VMEM((ny, lanes), f32),
        "ysr": pltpu.VMEM((ny, ny, lanes), f32),
        "ya": pltpu.VMEM((ny, lanes), f32),
        "fin": pltpu.VMEM((8, lanes), f32),
        "zfr": pltpu.VMEM((nz, 8, lanes), f32),
        "gqy": pltpu.VMEM((ny, lanes, width), f32),
        "gqz": pltpu.VMEM((nz, lanes, width), f32),
        "chain": pltpu.VMEM((nx + CORES, max(ny, nz) + 1, rows, width), f32),
        "own": pltpu.VMEM((owned, rows, width), f32),
        "yo": pltpu.VMEM((max(ny - 1, 1) * qb, rows, width), bf),
        "yi": pltpu.VMEM((max(ny - 1, 1) * qb, rows, width), bf),
        "zo": pltpu.VMEM((max(nz - 1, 1) * qb, rows, width), bf),
        "zi": pltpu.VMEM((max(nz - 1, 1) * qb, rows, width), bf),
        "xo": pltpu.VMEM((max(nx - 1, 1) * owned, rows, width), bf),
        "xi": pltpu.VMEM((max(nx - 1, 1) * owned, rows, width), bf),
        "co": pltpu.VMEM((owned, rows, width), bf),
        "ci": pltpu.VMEM((owned, rows, width), bf),
        "gqo": pltpu.VMEM((qb, rows, width), bf),
        "gpo": pltpu.VMEM((owned, rows, width), bf),
        "p0": pltpu.VMEM((owned, rows, width), bf),
        "cand": pltpu.SMEM(cand_shape, jnp.int32),
        "map": pltpu.SMEM(map_shape, jnp.int32),
        "posv": pltpu.VMEM((qb, rows), jnp.int32),
        "wv": pltpu.VMEM((qb, rows), f32),
        "links": pltpu.SMEM(((nx + CORES) * (max(ny, nz) + owned),), jnp.int32),
        "sent": dma((13,)),
        "got": dma((8,)),
        "near": dma((7,)),
        "yr": dma((max(ny - 1, 1) * qb,)),
        "zr": dma((max(nz - 1, 1) * qb,)),
        "xr": dma((max(nx - 1, 1) * owned,)),
        "xr2": dma((max(nx - 1, 1) * owned,)),
    }
    for h in range(1, nx):
        plan[f"px{h}"] = pltpu.VMEM((owned, rows, width), bf)
    return plan


def kernel(sizes, names, q_ref, p_ref, cand_ref, own_ref, pos_ref, w_ref, gq_ref, gp_ref, *scratch):
    nx, ny, nz = sizes
    s = dict(zip(names, scratch))
    qb, rows, width = q_ref.shape
    owned = p_ref.shape[0]
    ncand = cand_ref.shape[0]
    lanes = qb * rows
    scale = 3.0 / math.sqrt(width)
    dp_size = nx * ny
    g, dp = lax.axis_index("group"), lax.axis_index("dp")
    x, y = dp // ny, dp % ny
    z, c = g // CORES, g % CORES

    def at_y(r):
        return (g, x * ny + (y + r) % ny)

    def at_x(r):
        return (g, ((x + r) % nx) * ny + y)

    def at_z(r):
        return (((z + r) % nz) * CORES + c, dp)

    partner = (z * CORES + (1 - c), dp)

    peers = [at_y(r) for r in range(1, ny)] + [at_z(r) for r in range(1, nz)] + [partner]
    peers += [at_x(r) for r in sorted({1 % nx, (nx - 1) % nx} - {0})]
    def fetch(src, dst, sem):
        copy = pltpu.make_async_copy(src, dst, s["near"].at[sem])
        copy.start()
        return copy

    scalars = [fetch(cand_ref, s["cand"], 0), fetch(own_ref, s["map"], 1)]
    rows_in = [fetch(pos_ref, s["posv"], 2), fetch(w_ref, s["wv"], 3)]
    barrier = pltpu.get_barrier_semaphore()
    for peer in peers:
        pl.semaphore_signal(barrier, inc=1, device_id=peer, device_id_type=MESH)
    pl.semaphore_wait(barrier, len(peers))

    def send(src, dst, family, recv_sem, device):
        return pltpu.make_async_remote_copy(
            src_ref=src,
            dst_ref=dst,
            send_sem=s["sent"].at[family],
            recv_sem=recv_sem,
            device_id=device,
            device_id_type=MESH,
        )

    def start(copy):
        copy.start()

    def all_sent(family, extent):
        send(extent, extent, family, s["got"].at[7], partner).wait_send()

    def stream(kind, parts):
        return [
            (way, part)
            for part in range(parts)
            for way in (0, 1)
            if ((part >= parts // 2) == (way == 1)) == (kind == "A")
        ]

    def steps(n, kind):
        return n // 2 - (kind == "B")

    def slots(n, way, t):
        return ((-t) % n, (-(t + 1)) % n) if way == 0 else (t, t + 1)

    def entry(n, parts, way, t, part):
        half = n // 2
        return (2 * t + way) * parts + part if t < half - 1 else 2 * (half - 1) * parts + part

    def query_copy(line, n, device_at, way, t, part):
        src, dst = slots(n, way, t)
        buf = s["q" + line]
        block = pl.ds(part * rows, rows)
        return send(
            q_ref.at[part] if t == 0 else buf.at[src, block],
            buf.at[dst, block],
            "yz".index(line),
            s[line + "r"].at[entry(n, qb, way, t, part)],
            device_at(1 if way == 0 else n - 1),
        )

    def y_copy(way, t, part):
        return query_copy("y", ny, at_y, way, t, part)

    def z_copy(way, t, part):
        return query_copy("z", nz, at_z, way, t, part)

    passages = [s["p0"]] + [s[f"px{h}"] for h in range(1, nx)]

    def x_copy(way, t, part):
        src, dst = slots(nx, way, t)
        return send(
            p_ref.at[part] if t == 0 else passages[src].at[part],
            passages[dst].at[part],
            2,
            s["xr"].at[entry(nx, owned, way, t, part)],
            at_x(1 if way == 0 else nx - 1),
        )

    rings = {"y": (ny, y_copy, qb), "z": (nz, z_copy, qb), "x": (nx, x_copy, owned)}

    def launch(line, kind, t):
        n, copy, parts = rings[line]
        if t < steps(n, kind):
            for way, part in stream(kind, parts):
                start(copy(way, t, part))

    def land(line, kind, t):
        n, copy, parts = rings[line]
        if t < steps(n, kind):
            for way, part in stream(kind, parts):
                copy(way, t, part).wait_recv()

    def relay(kind, t):
        for line in "yz":
            land(line, kind, t - 1)
            launch(line, kind, t)

    for line in "yzx":
        launch(line, "A", 0)
    core_gather = send(p_ref, s["pc"], 3, s["got"].at[0], partner)
    start(core_gather)

    whole_q = [fetch(q_ref.at[b], s["qy"].at[0, pl.ds(b * rows, rows)], 4 + b) for b in range(qb)]
    whole_p = fetch(p_ref, s["p0"], 4 + qb)
    for copy in rows_in:
        copy.wait()
    tile_row = lax.broadcasted_iota(jnp.int32, (8, lanes), 0)
    w_row = jnp.concatenate([s["wv"][b : b + 1, :] for b in range(qb)], axis=1) * scale
    pos_row = jnp.concatenate([s["posv"][b : b + 1, :] for b in range(qb)], axis=1).astype(jnp.float32)
    own_aux = jnp.where(tile_row == 0, w_row, jnp.where(tile_row == 1, pos_row, 0.0))
    s["auxy"][0] = own_aux
    s["auxz"][0] = own_aux

    def spread(n, device_at, src, dst, family):
        for r in range(1, n):
            start(send(src, dst.at[n - r], family, s["got"].at[family - 3], device_at(r)))

        def wait():
            if n > 1:
                extent = dst.at[pl.ds(1, n - 1)]
                send(extent, extent, family, s["got"].at[family - 3], partner).wait_recv()

        return wait

    def entry_y(h, r):
        return (h * ny + r) * 3

    def entry_z(h, r):
        return (nx * ny + h * nz + r) * 3

    def fill(lister, holders, entries):
        found = [jnp.int32(0)] * len(holders)
        for b in range(qb):
            listing = [jnp.int32(-1)] * len(holders)
            for k in range(ncand):
                place = s["map"][s["cand"][k, lister * qb + b]]
                for i, holder in enumerate(holders):
                    offset = place - holder * owned
                    hit = offset.astype(jnp.uint32) < jnp.uint32(owned)
                    listing[i] = jnp.where(hit, k, listing[i])
                    found[i] = jnp.where(hit, offset, found[i])
            for i, entry in enumerate(entries):
                s["tab"][entry + b] = listing[i]
        for i, entry in enumerate(entries):
            s["tab"][entry + 2] = found[i]

    def fill_y(r, carry):
        holders = [g * dp_size + ((x + h) % nx) * ny + y for h in range(nx)]
        fill(g * dp_size + x * ny + (y + r) % ny, holders, [entry_y(h, r) for h in range(nx)])
        return carry

    def fill_z(r, carry):
        own = jnp.where(r == 0, -1000, g * dp_size + dp)
        other = (z * CORES + (1 - c)) * dp_size + dp
        fill((((z + r) % nz) * CORES + c) * dp_size + dp, [own, other], [entry_z(h, r) for h in range(CORES)])
        return carry

    for copy in scalars:
        copy.wait()
    lax.fori_loop(0, nz, fill_z, 0)
    for line in "yz":
        launch(line, "B", 0)
    for copy in whole_q:
        copy.wait()
    s["qz"][0] = s["qy"][0]
    whole_p.wait()
    aux_y = spread(ny, at_y, s["auxy"].at[0], s["auxy"], 4)
    aux_z = spread(nz, at_z, s["auxz"].at[0], s["auxz"], 5)

    lane = lax.broadcasted_iota(jnp.int32, (1, lanes), 1)

    def listing_row(entry):
        row = jnp.full((1, lanes), s["tab"][entry], jnp.int32)
        for b in range(1, qb):
            row = jnp.where(lane >= b * rows, s["tab"][entry + b], row)
        return row

    def score(pairs, q):
        blocks = [held[s["tab"][where + 2]] for held, where, _, _, _ in pairs]
        block = jnp.concatenate(blocks, axis=0) if len(blocks) > 1 else blocks[0]
        joined = lax.dot_general(block, q, (((1,), (1,)), ((), ())), preferred_element_type=jnp.float32) * scale
        for i, (_, where, index, (top_ref, lse_ref, h), r) in enumerate(pairs):
            scores = joined[i * rows : (i + 1) * rows]
            scores = jnp.where(listing_row(where) >= 0, scores, NEG)
            top = jnp.max(scores, axis=0, keepdims=True)
            powers = jnp.exp(scores - top)
            s["e"][index] = powers
            top_ref[h, pl.ds(r, 1), :] = top
            lse_ref[h, pl.ds(r, 1), :] = top + jnp.log(jnp.sum(powers, axis=0, keepdims=True))

    def score_y(hs, r):
        score([(passages[h], entry_y(h, r), h * ny + r, (s["my"], s["sy"], h), r) for h in hs], s["qy"][r])

    held_z = [s["p0"], s["pc"]]

    def score_z(r):
        pairs = [(held_z[h], entry_z(h, r), nx * ny + h * nz + r, (s["mz"], s["sz"], h), r) for h in range(CORES)]
        score(pairs, s["qz"][r])

    def each(count, first_slot, n, body):
        def step(i, carry):
            body((i + first_slot) % n)
            return carry

        lax.fori_loop(0, count, step, 0)

    half_y, half_z, half_x = ny // 2, nz // 2, nx // 2
    near_y, near_z = max(half_y - 2, 0), max(half_z - 2, 0)
    relay("A", 1)
    lax.fori_loop(0, ny // 2, fill_y, 0)
    relay("B", 1)
    launch("x", "B", 0)
    lax.fori_loop(ny // 2, ny, fill_y, 0)
    relay("A", 2)
    for t in range(1, half_x):
        land("x", "A", t - 1)
        launch("x", "A", t)

    span = max(ny, nz) + owned
    for h in range(nx + CORES):
        n = ny if h < nx else nz
        found = [s["tab"][(entry_y(h, r) if h < nx else entry_z(h - nx, r)) + 2] for r in range(n)]
        for r in range(n):
            before = jnp.int32(0)
            for other in range(r):
                before = jnp.where(found[other] == found[r], other + 1, before)
            s["links"][h * span + r] = before
        for p in range(owned):
            last = jnp.int32(0)
            for r in range(n):
                last = jnp.where(found[r] == p, r + 1, last)
            s["links"][h * span + max(ny, nz) + p] = last
        s["chain"][h, 0] = jnp.zeros((rows, width), jnp.float32)

    relay("B", 2)
    core_gather.wait_recv()
    each(2 * near_z + 1, nz - near_z, nz, score_z)
    relay("A", 3)
    each(2 * near_y + 1, ny - near_y, ny, lambda r: score_y([0], r))
    relay("B", 3)
    relay("A", 4)
    each(nz - 2 * near_z - 1, near_z + 1, nz, score_z)

    def merge(parts):
        top = functools.reduce(jnp.maximum, parts)
        return top + jnp.log(sum(jnp.exp(part - top) for part in parts))

    s["zst"][...] = merge([s["sz"][h] for h in range(CORES)])
    stat_z = spread(nz, at_z, s["zst"], s["zsr"], 6)
    each(ny - 2 * near_y - 1, near_y + 1, ny, lambda r: score_y([0], r))

    for t in range(half_x - 1):
        land("x", "B", t)
    middle = [h for h in range(1, nx) if h != half_x]

    if middle:
        each(ny, 0, ny, lambda r: score_y(middle, r))
    own_z = [s["zst"][0:1, :]]
    stat_z()
    own_z += [s["zsr"][j][nz - j : nz - j + 1, :] for j in range(1, nz)]
    z_row = merge(own_z)
    if nx > 1:
        land("x", "A", half_x - 1)

        def last_pairs(i):
            score_y([half_x], i)
            score_y([half_x], i + ny // 2)

        each(ny // 2, 0, ny, last_pairs)

    stat = merge([s["sy"][h] for h in range(nx)])
    ring_row = lax.broadcasted_iota(jnp.int32, (ny, lanes), 0)
    stat = jnp.where(ring_row == 0, merge([stat, jnp.broadcast_to(z_row, stat.shape)]), stat)
    s["yst"][...] = stat
    stat_y = spread(ny, at_y, s["yst"], s["ysr"], 7)
    aux_y()
    aux_z()
    stat_y()

    def turned(value, places):
        if ny == 8:
            return pltpu.roll(value, places, axis=0)
        return jnp.concatenate([value[ny - places :], value[: ny - places]], axis=0)

    total = merge([stat] + [turned(s["ysr"][j], j) for j in range(1, ny)])
    s["ya"][...] = total
    s["fin"][...] = jnp.broadcast_to(total[0:1, :], (8, lanes))
    fin_z = spread(nz, at_z, s["fin"], s["zfr"], 8)

    down = lax.broadcasted_iota(jnp.int32, (rows, lanes), 0).astype(jnp.float32)

    def dscore(index, entry, m_row, a_row, w_line, pos_line):
        factor = jnp.exp(m_row - a_row) * w_line
        spot = pos_line - (listing_row(entry) * rows).astype(jnp.float32)
        value = s["e"][index] * factor - jnp.where(down == spot, w_line, 0.0)
        s["d"][index] = value.astype(jnp.bfloat16)

    def dscore_y(h, r):
        dscore(
            h * ny + r,
            entry_y(h, r),
            s["my"][h, pl.ds(r, 1), :],
            s["ya"][pl.ds(r, 1), :],
            s["auxy"][r, 0:1, :],
            s["auxy"][r, 1:2, :],
        )

    def dscore_z(h, r, a_row):
        dscore(
            nx * ny + h * nz + r,
            entry_z(h, r),
            s["mz"][h, pl.ds(r, 1), :],
            a_row,
            s["auxz"][r, 0:1, :],
            s["auxz"][r, 1:2, :],
        )

    def term(h, r, index, q):
        value = jnp.dot(s["d"][index], q, preferred_element_type=jnp.float32)
        s["chain"][h, r + 1] = value + s["chain"][h, s["links"][h * span + r]]

    def block_sum(h, p):
        return s["chain"][h, s["links"][h * span + max(ny, nz) + p]]

    def query_part(out, r, pairs):
        left = jnp.concatenate([s["d"][index] for index, _, _ in pairs], axis=0)
        right = jnp.concatenate([held[s["tab"][where + 2]] for _, held, where in pairs], axis=0)
        out[r] = lax.dot_general(left, right, (((0,), (0,)), ((), ())), preferred_element_type=jnp.float32)

    def reduce_copy(line, n, device_at, way, t, part):
        place = entry(n, owned if line == "x" else qb, way, t - 1, part)
        return send(
            s[line + "o"].at[place],
            s[line + "i"].at[place],
            9 + "yzx".index(line),
            s["xr2" if line == "x" else line + "r"].at[place],
            device_at(1 if way == 0 else n - 1),
        )

    def came(line, n, way, t, part):
        return s[line + "i"][entry(n, owned if line == "x" else qb, way, t - 1, part)].astype(jnp.float32)

    def reduce_send(line, n, device_at, way, t, part, value, alone):
        if not alone:
            reduce_copy(line, n, device_at, way, t + 1, part).wait_recv()
            value = value + came(line, n, way, t + 1, part)
        s[line + "o"][entry(n, owned if line == "x" else qb, way, t - 1, part)] = value.astype(jnp.bfloat16)
        start(reduce_copy(line, n, device_at, way, t, part))

    def query_send(line, kind, t):
        n, device_at = (ny, at_y) if line == "y" else (nz, at_z)
        if 1 <= t <= steps(n, kind):
            for way, part in stream(kind, qb):
                target = t if way == 0 else (n - t) % n
                value = s["gq" + line][target, pl.ds(part * rows, rows), :]
                reduce_send(line, n, device_at, way, t, part, value, t == steps(n, kind))

    def passage_send(kind, t):
        if 1 <= t <= steps(nx, kind):
            for way, part in stream(kind, owned):
                target = t if way == 0 else (nx - t) % nx
                reduce_send("x", nx, at_x, way, t, part, block_sum(target, part), t == steps(nx, kind))

    def grad_x(h, fresh):
        def pair(r):
            if fresh:
                dscore_y(h, r)
            term(h, r, h * ny + r, s["qy"][r])

        each(ny, 0, ny, pair)

    if nx > 1:
        grad_x(half_x, True)
        passage_send("A", half_x)
    rest = [h for h in range(nx) if nx == 1 or h != half_x]

    def query_y(hs):
        def body(r):
            for h in hs:
                dscore_y(h, r)
            query_part(s["gqy"], r, [(h * ny + r, passages[h], entry_y(h, r)) for h in range(nx)])

        return body

    def query_z(r):
        a_row = s["zfr"][r, 0:1, :]
        for h in range(CORES):
            dscore_z(h, r, a_row)
        query_part(s["gqz"], r, [(nx * ny + h * nz + r, held_z[h], entry_z(h, r)) for h in range(CORES)])

    def grad_z(h):
        each(nz, 0, nz, lambda r: term(nx + h, r, nx * ny + h * nz + r, s["qz"][r]))

    def targets(n, body, group):
        half = n // 2
        if group == 0:
            each(1, half, n, body)
        elif group == 3 and n > 1:
            each(min(3, n - 1), n - 1 if n > 2 else 0, n, body)
        elif group in (1, 2) and n > 2:
            each(2, 0, 2, lambda i: body(half - group + 2 * group * i))

    assert ny in (1, 2, 8) and nz in (1, 2, 8)
    targets(ny, query_y(rest), 0)
    query_send("y", "A", half_y)
    for h in middle[:1]:
        grad_x(h, True)
    rest = [h for h in rest if h not in middle[:1]]
    targets(ny, query_y(rest), 1)
    query_send("y", "B", half_y - 1)
    for h in middle[1:]:
        grad_x(h, True)
    rest = [h for h in rest if h not in middle]
    targets(ny, query_y(rest), 2)
    fin_z()
    s["zfr"][0] = s["fin"][...]
    targets(nz, query_z, 0)
    query_send("z", "A", half_z)
    query_send("y", "A", half_y - 1)
    targets(nz, query_z, 1)
    query_send("z", "B", half_z - 1)
    for t in range(half_x - 1, 0, -1):
        passage_send("B", t)
    targets(ny, query_y(rest), 3)
    query_send("y", "B", half_y - 2)
    targets(nz, query_z, 2)
    targets(nz, query_z, 3)
    query_send("z", "A", half_z - 1)
    query_send("y", "A", half_y - 2)
    query_send("z", "B", half_z - 2)
    grad_z(1)
    for part in range(owned):
        s["co"][part] = block_sum(nx + 1, part).astype(jnp.bfloat16)
    core_reduce = send(s["co"], s["ci"], 12, s["got"].at[6], partner)
    start(core_reduce)
    query_send("y", "B", half_y - 3)
    for t in range(half_x - 1, 0, -1):
        passage_send("A", t)
    query_send("z", "A", half_z - 2)
    query_send("y", "A", half_y - 3)
    query_send("z", "B", half_z - 3)
    grad_z(0)
    grad_x(0, False)
    query_send("z", "A", half_z - 3)

    def arrived(line, n, device_at, parts, part):
        total = None
        for way in (0, 1):
            if n > 2 or (n == 2 and (way, part) in stream("A", parts)):
                reduce_copy(line, n, device_at, way, 1, part).wait_recv()
                value = came(line, n, way, 1, part)
                total = value if total is None else total + value
        return 0.0 if total is None else total

    core_reduce.wait_recv()
    for part in range(owned):
        s["own"][part] = block_sum(0, part) + block_sum(nx, part) + s["ci"][part].astype(jnp.float32)
    results = []
    for part in range(qb):
        block = pl.ds(part * rows, rows)
        value = s["gqy"][0, block, :] + s["gqz"][0, block, :]
        value += arrived("y", ny, at_y, qb, part)
        value += arrived("z", nz, at_z, qb, part)
        s["gqo"][part] = value.astype(gq_ref.dtype)
    results.append(fetch(s["gqo"], gq_ref, 0))
    for part in range(owned):
        value = s["own"][part] + arrived("x", nx, at_x, owned, part)
        s["gpo"][part] = value.astype(gp_ref.dtype)
        results.append(fetch(s["gpo"].at[part], gp_ref.at[part], 1 + part))
    if ny > 1:
        for family, extent in ((0, s["yo"]), (9, s["yo"]), (4, s["auxy"].at[pl.ds(1, ny - 1)]), (7, s["ysr"].at[pl.ds(1, ny - 1)])):
            all_sent(family, extent)
    if nz > 1:
        for family, extent in ((1, s["zo"]), (10, s["zo"]), (5, s["auxz"].at[pl.ds(1, nz - 1)])):
            all_sent(family, extent)
        for family, extent in ((6, s["zsr"].at[pl.ds(1, nz - 1)]), (8, s["zfr"].at[pl.ds(1, nz - 1)])):
            all_sent(family, extent)
    if nx > 1:
        all_sent(2, s["xo"])
        all_sent(11, s["xo"])
    all_sent(3, s["pc"])
    all_sent(12, s["co"])
    for copy in results:
        copy.wait()


def hand_over(gq_in, gp_in, gq_out, gp_out, gq, gp, sems):
    pieces = [(gq_in, gq, gq_out, 0)] + [(gp_in, gp, gp_out, part) for part in range(gp_in.shape[0])]
    loads, stores = [], []
    for i, (src, held, dst, part) in enumerate(pieces):
        piece = slice(None) if i == 0 else pl.ds(part, 1)
        loads.append(pltpu.make_async_copy(src.at[piece], held.at[piece], sems.at[0, i]))
        stores.append(pltpu.make_async_copy(held.at[piece], dst.at[piece], sems.at[1, i]))
    for load in loads:
        load.start()
    for load, store in zip(loads, stores):
        load.wait()
        store.start()
    for store in stores:
        store.wait()


def solution(mesh, sizes=SIZES):
    nx, ny = sizes
    nz = mesh.shape["group"] // CORES
    assert mesh.shape["dp"] == nx * ny

    def shards(queries, passages, candidates, positives, row_weight, owner_map):
        listed = candidates.T
        plan = scratch_plan(nx, ny, nz, queries.shape[0], *passages.shape, listed.shape, owner_map.shape)
        left = pl.BlockSpec(memory_space=pl.ANY)
        shapes = (
            jax.ShapeDtypeStruct(queries.shape, queries.dtype),
            jax.ShapeDtypeStruct(passages.shape, passages.dtype),
        )
        results = pl.pallas_call(
            functools.partial(kernel, (nx, ny, nz), tuple(plan)),
            out_shape=shapes,
            in_specs=[left] * 6,
            out_specs=(left, left),
            scratch_shapes=list(plan.values()),
            compiler_params=pltpu.CompilerParams(
                collective_id=0, has_side_effects=True, vmem_limit_bytes=64_000_000
            ),
        )(queries, passages, listed, owner_map, positives, row_weight)
        return pl.pallas_call(
            hand_over,
            out_shape=shapes,
            in_specs=[left] * 2,
            out_specs=(left, left),
            scratch_shapes=[
                pltpu.VMEM(queries.shape, queries.dtype),
                pltpu.VMEM(passages.shape, passages.dtype),
                pltpu.SemaphoreType.DMA((2, passages.shape[0] + 1)),
            ],
        )(*results)

    return jax.shard_map(
        shards,
        mesh=mesh,
        in_specs=(
            P(("group", "dp"), None, None),
            P(("group", "dp"), None, None),
            P(),
            P(("group", "dp"), None),
            P(("group", "dp"), None),
            P(),
        ),
        out_specs=(P(("group", "dp"), None, None), P(("group", "dp"), None, None)),
        check_vma=False,
    )
```

```python
import functools
import math

import jax
import jax.numpy as jnp
from jax import lax
from jax.experimental import pallas as pl
from jax.experimental.pallas import tpu as pltpu
from jax.sharding import PartitionSpec as P

MESH = pl.DeviceIdType.MESH
NEG = -1e30
CORES = 2
CUTS = 2
SIZES = (4, 8)


def scratch_plan(nx, ny, nz, qb, owned, rows, width, cand_shape, map_shape):
    lanes, qp = qb * rows, qb * CUTS
    dma = pltpu.SemaphoreType.DMA
    bf, f32 = jnp.bfloat16, jnp.float32
    plan = {
        "qy": pltpu.VMEM((ny, lanes, width), bf),
        "qz": pltpu.VMEM((nz, lanes, width), bf),
        "pc": pltpu.VMEM((owned, rows, width), bf),
        "tab": pltpu.SMEM(((nx * ny + CORES * nz) * 3,), jnp.int32),
        "e": pltpu.VMEM((nx * ny + CORES * nz, rows, lanes), f32),
        "d": pltpu.VMEM((nx * ny + CORES * nz, rows, lanes), bf),
        "my": pltpu.VMEM((nx, ny, lanes), f32),
        "sy": pltpu.VMEM((nx, ny, lanes), f32),
        "mz": pltpu.VMEM((CORES, nz, lanes), f32),
        "sz": pltpu.VMEM((CORES, nz, lanes), f32),
        "zst": pltpu.VMEM((nz, lanes), f32),
        "zsr": pltpu.VMEM((nz, nz, lanes), f32),
        "yst": pltpu.VMEM((ny + 8, lanes), f32),
        "ysr": pltpu.VMEM((ny, ny + 8, lanes), f32),
        "ya": pltpu.VMEM((ny, lanes), f32),
        "fin": pltpu.VMEM((8, lanes), f32),
        "zfr": pltpu.VMEM((nz, 8, lanes), f32),
        "gqy": pltpu.VMEM((ny, lanes, width), f32),
        "gqz": pltpu.VMEM((nz, lanes, width), f32),
        "chain": pltpu.VMEM((nx + CORES, max(ny, nz) + 1, rows, width), f32),
        "own": pltpu.VMEM((owned, rows, width), f32),
        "yo": pltpu.VMEM((max(ny - 1, 1) * qp, lanes // qp, width), bf),
        "yi": pltpu.VMEM((max(ny - 1, 1) * qp, lanes // qp, width), bf),
        "zo": pltpu.VMEM((max(nz - 1, 1) * qp, lanes // qp, width), bf),
        "zi": pltpu.VMEM((max(nz - 1, 1) * qp, lanes // qp, width), bf),
        "xo": pltpu.VMEM((max(nx - 1, 1) * owned, rows, width), bf),
        "xi": pltpu.VMEM((max(nx - 1, 1) * owned, rows, width), bf),
        "co": pltpu.VMEM((owned, rows, width), bf),
        "ci": pltpu.VMEM((owned, rows, width), bf),
        "gqo": pltpu.VMEM((qb, rows, width), bf),
        "gpo": pltpu.VMEM((owned, rows, width), bf),
        "p0": pltpu.VMEM((owned, rows, width), bf),
        "cand": pltpu.SMEM(cand_shape, jnp.int32),
        "map": pltpu.SMEM(map_shape, jnp.int32),
        "posv": pltpu.VMEM((qb, rows), jnp.int32),
        "wv": pltpu.VMEM((qb, rows), f32),
        "links": pltpu.SMEM(((nx + CORES) * (max(ny, nz) + owned),), jnp.int32),
        "sent": dma((13,)),
        "got": dma((8,)),
        "near": dma((7,)),
        "yr": dma((max(ny - 1, 1) * qp,)),
        "zr": dma((max(nz - 1, 1) * qp,)),
        "xr": dma((max(nx - 1, 1) * owned,)),
        "xr2": dma((max(nx - 1, 1) * owned,)),
    }
    for h in range(1, nx):
        plan[f"px{h}"] = pltpu.VMEM((owned, rows, width), bf)
    return plan


def kernel(sizes, names, q_ref, p_ref, cand_ref, own_ref, pos_ref, w_ref, gq_ref, gp_ref, *scratch):
    nx, ny, nz = sizes
    s = dict(zip(names, scratch))
    qb, rows, width = q_ref.shape
    owned = p_ref.shape[0]
    ncand = cand_ref.shape[0]
    lanes, qp, piece = qb * rows, qb * CUTS, rows // CUTS
    scale = 3.0 / math.sqrt(width)
    dp_size = nx * ny
    g, dp = lax.axis_index("group"), lax.axis_index("dp")
    x, y = dp // ny, dp % ny
    z, c = g // CORES, g % CORES

    def at_y(r):
        return (g, x * ny + (y + r) % ny)

    def at_x(r):
        return (g, ((x + r) % nx) * ny + y)

    def at_z(r):
        return (((z + r) % nz) * CORES + c, dp)

    partner = (z * CORES + (1 - c), dp)

    peers = [at_y(r) for r in range(1, ny)] + [at_z(r) for r in range(1, nz)] + [partner]
    peers += [at_x(r) for r in sorted({1 % nx, (nx - 1) % nx} - {0})]
    def fetch(src, dst, sem):
        copy = pltpu.make_async_copy(src, dst, s["near"].at[sem])
        copy.start()
        return copy

    scalars = [fetch(cand_ref, s["cand"], 0), fetch(own_ref, s["map"], 1)]
    rows_in = [fetch(pos_ref, s["posv"], 2), fetch(w_ref, s["wv"], 3)]
    barrier = pltpu.get_barrier_semaphore()
    for peer in peers:
        pl.semaphore_signal(barrier, inc=1, device_id=peer, device_id_type=MESH)
    pl.semaphore_wait(barrier, len(peers))

    def send(src, dst, family, recv_sem, device):
        return pltpu.make_async_remote_copy(
            src_ref=src,
            dst_ref=dst,
            send_sem=s["sent"].at[family],
            recv_sem=recv_sem,
            device_id=device,
            device_id_type=MESH,
        )

    def start(copy):
        copy.start()

    def all_sent(family, extent):
        send(extent, extent, family, s["got"].at[7], partner).wait_send()

    def stream(kind, parts):
        return [
            (way, part)
            for part in range(parts)
            for way in (0, 1)
            if ((part >= parts // 2) == (way == 1)) == (kind == "A")
        ]

    def steps(n, kind):
        return n // 2 - (kind == "B")

    def slots(n, way, t):
        return ((-t) % n, (-(t + 1)) % n) if way == 0 else (t, t + 1)

    def entry(n, parts, way, t, part):
        half = n // 2
        return (2 * t + way) * parts + part if t < half - 1 else 2 * (half - 1) * parts + part

    def query_copy(line, n, device_at, way, t, part):
        src, dst = slots(n, way, t)
        buf = s["q" + line]
        block = pl.ds(part * piece, piece)
        return send(
            q_ref.at[part // CUTS, pl.ds(part % CUTS * piece, piece)] if t == 0 else buf.at[src, block],
            buf.at[dst, block],
            "yz".index(line),
            s[line + "r"].at[entry(n, qp, way, t, part)],
            device_at(1 if way == 0 else n - 1),
        )

    def y_copy(way, t, part):
        return query_copy("y", ny, at_y, way, t, part)

    def z_copy(way, t, part):
        return query_copy("z", nz, at_z, way, t, part)

    passages = [s["p0"]] + [s[f"px{h}"] for h in range(1, nx)]

    def x_copy(way, t, part):
        src, dst = slots(nx, way, t)
        return send(
            p_ref.at[part] if t == 0 else passages[src].at[part],
            passages[dst].at[part],
            2,
            s["xr"].at[entry(nx, owned, way, t, part)],
            at_x(1 if way == 0 else nx - 1),
        )

    rings = {"y": (ny, y_copy, qp), "z": (nz, z_copy, qp), "x": (nx, x_copy, owned)}

    def launch(line, kind, t):
        n, copy, parts = rings[line]
        if t < steps(n, kind):
            for way, part in stream(kind, parts):
                start(copy(way, t, part))

    def land(line, kind, t):
        n, copy, parts = rings[line]
        if t < steps(n, kind):
            for way, part in stream(kind, parts):
                copy(way, t, part).wait_recv()

    def relay(kind, t):
        for way, part in stream(kind, qp):
            for line in "yz":
                n, copy, _ = rings[line]
                if t - 1 < steps(n, kind):
                    copy(way, t - 1, part).wait_recv()
                if t < steps(n, kind):
                    start(copy(way, t, part))

    for kind in "AB":
        for line in "yzx":
            launch(line, kind, 0)
    core_gather = send(p_ref, s["pc"], 3, s["got"].at[0], partner)
    start(core_gather)

    whole_q = [fetch(q_ref.at[b], s["qy"].at[0, pl.ds(b * rows, rows)], 4 + b) for b in range(qb)]
    whole_p = fetch(p_ref, s["p0"], 4 + qb)
    for copy in rows_in:
        copy.wait()
    tile_row = lax.broadcasted_iota(jnp.int32, (8, lanes), 0)
    w_row = jnp.concatenate([s["wv"][b : b + 1, :] for b in range(qb)], axis=1) * scale
    pos_row = jnp.concatenate([s["posv"][b : b + 1, :] for b in range(qb)], axis=1).astype(jnp.float32)
    s["yst"][ny : ny + 8] = jnp.where(tile_row == 0, w_row, jnp.where(tile_row == 1, pos_row, 0.0))

    def spread(n, device_at, src, dst, family):
        for r in range(1, n):
            start(send(src, dst.at[n - r], family, s["got"].at[family - 3], device_at(r)))

        def wait():
            if n > 1:
                extent = dst.at[pl.ds(1, n - 1)]
                send(extent, extent, family, s["got"].at[family - 3], partner).wait_recv()

        return wait

    def entry_y(h, r):
        return (h * ny + r) * 3

    def entry_z(h, r):
        return (nx * ny + h * nz + r) * 3

    def fill(lister, holders, entries):
        found = [jnp.int32(0)] * len(holders)
        for b in range(qb):
            listing = [jnp.int32(-1)] * len(holders)
            for k in range(ncand):
                place = s["map"][s["cand"][k, lister * qb + b]]
                for i, holder in enumerate(holders):
                    offset = place - holder * owned
                    hit = offset.astype(jnp.uint32) < jnp.uint32(owned)
                    listing[i] = jnp.where(hit, k, listing[i])
                    found[i] = jnp.where(hit, offset, found[i])
            for i, entry in enumerate(entries):
                s["tab"][entry + b] = listing[i]
        for i, entry in enumerate(entries):
            s["tab"][entry + 2] = found[i]

    def fill_y(r, carry):
        holders = [g * dp_size + ((x + h) % nx) * ny + y for h in range(nx)]
        fill(g * dp_size + x * ny + (y + r) % ny, holders, [entry_y(h, r) for h in range(nx)])
        return carry

    def fill_z(r, carry):
        own = jnp.where(r == 0, -1000, g * dp_size + dp)
        other = (z * CORES + (1 - c)) * dp_size + dp
        fill((((z + r) % nz) * CORES + c) * dp_size + dp, [own, other], [entry_z(h, r) for h in range(CORES)])
        return carry

    for copy in scalars:
        copy.wait()
    lax.fori_loop(0, nz, fill_z, 0)
    for copy in whole_q:
        copy.wait()
    s["qz"][0] = s["qy"][0]
    whole_p.wait()

    lane = lax.broadcasted_iota(jnp.int32, (1, lanes), 1)

    def listing_row(entry):
        row = jnp.full((1, lanes), s["tab"][entry], jnp.int32)
        for b in range(1, qb):
            row = jnp.where(lane >= b * rows, s["tab"][entry + b], row)
        return row

    def score(pairs, q):
        blocks = [held[s["tab"][where + 2]] for held, where, _, _, _ in pairs]
        block = jnp.concatenate(blocks, axis=0) if len(blocks) > 1 else blocks[0]
        joined = lax.dot_general(block, q, (((1,), (1,)), ((), ())), preferred_element_type=jnp.float32) * scale
        for i, (_, where, index, (top_ref, lse_ref, h), r) in enumerate(pairs):
            scores = joined[i * rows : (i + 1) * rows]
            scores = jnp.where(listing_row(where) >= 0, scores, NEG)
            top = jnp.max(scores, axis=0, keepdims=True)
            powers = jnp.exp(scores - top)
            s["e"][index] = powers
            top_ref[h, pl.ds(r, 1), :] = top
            lse_ref[h, pl.ds(r, 1), :] = top + jnp.log(jnp.sum(powers, axis=0, keepdims=True))

    def score_y(hs, r):
        score([(passages[h], entry_y(h, r), h * ny + r, (s["my"], s["sy"], h), r) for h in hs], s["qy"][r])

    held_z = [s["p0"], s["pc"]]

    def score_z(r):
        pairs = [(held_z[h], entry_z(h, r), nx * ny + h * nz + r, (s["mz"], s["sz"], h), r) for h in range(CORES)]
        score(pairs, s["qz"][r])

    def each(count, first_slot, n, body):
        def step(i, carry):
            body((i + first_slot) % n)
            return carry

        lax.fori_loop(0, count, step, 0)

    half_y, half_z, half_x = ny // 2, nz // 2, nx // 2
    near_y, near_z = max(half_y - 2, 0), max(half_z - 2, 0)
    relay("A", 1)
    lax.fori_loop(0, ny // 2, fill_y, 0)
    relay("B", 1)
    lax.fori_loop(ny // 2, ny, fill_y, 0)
    relay("A", 2)
    for t in range(1, half_x):
        land("x", "A", t - 1)
        launch("x", "A", t)

    span = max(ny, nz) + owned
    for h in range(nx + CORES):
        n = ny if h < nx else nz
        found = [s["tab"][(entry_y(h, r) if h < nx else entry_z(h - nx, r)) + 2] for r in range(n)]
        for r in range(n):
            before = jnp.int32(0)
            for other in range(r):
                before = jnp.where(found[other] == found[r], other + 1, before)
            s["links"][h * span + r] = before
        for p in range(owned):
            last = jnp.int32(0)
            for r in range(n):
                last = jnp.where(found[r] == p, r + 1, last)
            s["links"][h * span + max(ny, nz) + p] = last
        s["chain"][h, 0] = jnp.zeros((rows, width), jnp.float32)

    relay("B", 2)
    core_gather.wait_recv()
    each(2 * near_z + 1, nz - near_z, nz, score_z)
    relay("A", 3)
    each(2 * near_y + 1, ny - near_y, ny, lambda r: score_y([0], r))
    relay("B", 3)
    relay("A", 4)
    each(nz - 2 * near_z - 1, near_z + 1, nz, score_z)

    def merge(parts):
        top = functools.reduce(jnp.maximum, parts)
        return top + jnp.log(sum(jnp.exp(part - top) for part in parts))

    s["zst"][...] = merge([s["sz"][h] for h in range(CORES)])
    stat_z = spread(nz, at_z, s["zst"], s["zsr"], 6)
    each(ny - 2 * near_y - 1, near_y + 1, ny, lambda r: score_y([0], r))

    for t in range(half_x - 1):
        land("x", "B", t)
    middle = [h for h in range(1, nx) if h != half_x]

    if middle:
        each(ny, 0, ny, lambda r: score_y(middle, r))
    own_z = [s["zst"][0:1, :]]
    stat_z()
    own_z += [s["zsr"][j][nz - j : nz - j + 1, :] for j in range(1, nz)]
    z_row = merge(own_z)
    if nx > 1:
        land("x", "A", half_x - 1)

        def last_pairs(i):
            score_y([half_x], i)
            score_y([half_x], i + ny // 2)

        each(ny // 2, 0, ny, last_pairs)

    stat = merge([s["sy"][h] for h in range(nx)])
    ring_row = lax.broadcasted_iota(jnp.int32, (ny, lanes), 0)
    stat = jnp.where(ring_row == 0, merge([stat, jnp.broadcast_to(z_row, stat.shape)]), stat)
    s["yst"][0:ny] = stat
    stat_y = spread(ny, at_y, s["yst"], s["ysr"], 7)
    stat_y()

    def turned(value, places):
        if ny == 8:
            return pltpu.roll(value, places, axis=0)
        return jnp.concatenate([value[ny - places :], value[: ny - places]], axis=0)

    total = merge([stat] + [turned(s["ysr"][j, 0:ny], j) for j in range(1, ny)])
    s["ya"][...] = total
    w_row, pos_row = s["yst"][ny : ny + 1, :], s["yst"][ny + 1 : ny + 2, :]
    fin = jnp.where(tile_row == 1, w_row, jnp.where(tile_row == 2, pos_row, 0.0))
    s["fin"][...] = jnp.where(tile_row == 0, total[0:1, :], fin)
    fin_z = spread(nz, at_z, s["fin"], s["zfr"], 8)

    s["ysr"][0] = s["yst"][...]

    down = lax.broadcasted_iota(jnp.int32, (rows, lanes), 0).astype(jnp.float32)

    def dscore(index, entry, m_row, a_row, w_line, pos_line):
        factor = jnp.exp(m_row - a_row) * w_line
        spot = pos_line - (listing_row(entry) * rows).astype(jnp.float32)
        value = s["e"][index] * factor - jnp.where(down == spot, w_line, 0.0)
        s["d"][index] = value.astype(jnp.bfloat16)

    def dscore_y(h, r):
        dscore(
            h * ny + r,
            entry_y(h, r),
            s["my"][h, pl.ds(r, 1), :],
            s["ya"][pl.ds(r, 1), :],
            s["ysr"][r, ny : ny + 1, :],
            s["ysr"][r, ny + 1 : ny + 2, :],
        )

    def dscore_z(h, r, a_row):
        dscore(
            nx * ny + h * nz + r,
            entry_z(h, r),
            s["mz"][h, pl.ds(r, 1), :],
            a_row,
            s["zfr"][r, 1:2, :],
            s["zfr"][r, 2:3, :],
        )

    def term(h, r, index, q):
        value = jnp.dot(s["d"][index], q, preferred_element_type=jnp.float32)
        s["chain"][h, r + 1] = value + s["chain"][h, s["links"][h * span + r]]

    def block_sum(h, p):
        return s["chain"][h, s["links"][h * span + max(ny, nz) + p]]

    def query_part(out, r, pairs):
        left = jnp.concatenate([s["d"][index] for index, _, _ in pairs], axis=0)
        right = jnp.concatenate([held[s["tab"][where + 2]] for _, held, where in pairs], axis=0)
        out[r] = lax.dot_general(left, right, (((0,), (0,)), ((), ())), preferred_element_type=jnp.float32)

    def reduce_copy(line, n, device_at, way, t, part):
        place = entry(n, owned if line == "x" else qp, way, t - 1, part)
        return send(
            s[line + "o"].at[place],
            s[line + "i"].at[place],
            9 + "yzx".index(line),
            s["xr2" if line == "x" else line + "r"].at[place],
            device_at(1 if way == 0 else n - 1),
        )

    def came(line, n, way, t, part):
        return s[line + "i"][entry(n, owned if line == "x" else qp, way, t - 1, part)].astype(jnp.float32)

    def reduce_send(line, n, device_at, way, t, part, value, alone):
        if not alone:
            reduce_copy(line, n, device_at, way, t + 1, part).wait_recv()
            value = value + came(line, n, way, t + 1, part)
        s[line + "o"][entry(n, owned if line == "x" else qp, way, t - 1, part)] = value.astype(jnp.bfloat16)
        start(reduce_copy(line, n, device_at, way, t, part))

    def query_send(line, kind, t):
        n, device_at = (ny, at_y) if line == "y" else (nz, at_z)
        if 1 <= t <= steps(n, kind):
            for way, part in stream(kind, qp):
                target = t if way == 0 else (n - t) % n
                value = s["gq" + line][target, pl.ds(part * piece, piece), :]
                reduce_send(line, n, device_at, way, t, part, value, t == steps(n, kind))

    def passage_send(kind, t):
        if 1 <= t <= steps(nx, kind):
            for way, part in stream(kind, owned):
                target = t if way == 0 else (nx - t) % nx
                reduce_send("x", nx, at_x, way, t, part, block_sum(target, part), t == steps(nx, kind))

    def grad_x(h, fresh):
        def pair(r):
            if fresh:
                dscore_y(h, r)
            term(h, r, h * ny + r, s["qy"][r])

        each(ny, 0, ny, pair)

    if nx > 1:
        grad_x(half_x, True)
        passage_send("A", half_x)
    rest = [h for h in range(nx) if nx == 1 or h != half_x]

    def query_y(hs):
        def body(r):
            for h in hs:
                dscore_y(h, r)
            query_part(s["gqy"], r, [(h * ny + r, passages[h], entry_y(h, r)) for h in range(nx)])

        return body

    def query_z(r):
        a_row = s["zfr"][r, 0:1, :]
        for h in range(CORES):
            dscore_z(h, r, a_row)
        query_part(s["gqz"], r, [(nx * ny + h * nz + r, held_z[h], entry_z(h, r)) for h in range(CORES)])

    def grad_z(h):
        each(nz, 0, nz, lambda r: term(nx + h, r, nx * ny + h * nz + r, s["qz"][r]))

    def targets(n, body, group):
        half = n // 2
        if group == 0:
            each(1, half, n, body)
        elif group == 3 and n > 1:
            each(min(3, n - 1), n - 1 if n > 2 else 0, n, body)
        elif group in (1, 2) and n > 2:
            each(2, 0, 2, lambda i: body(half - group + 2 * group * i))

    assert ny in (1, 2, 8) and nz in (1, 2, 8)
    targets(ny, query_y(rest), 0)
    query_send("y", "A", half_y)
    for h in middle[:1]:
        grad_x(h, True)
    rest = [h for h in rest if h not in middle[:1]]
    targets(ny, query_y(rest), 1)
    query_send("y", "B", half_y - 1)
    for h in middle[1:]:
        grad_x(h, True)
    rest = [h for h in rest if h not in middle]
    targets(ny, query_y(rest), 2)
    fin_z()
    s["zfr"][0] = s["fin"][...]
    targets(nz, query_z, 0)
    query_send("z", "A", half_z)
    query_send("y", "A", half_y - 1)
    targets(nz, query_z, 1)
    query_send("z", "B", half_z - 1)
    for t in range(half_x - 1, 0, -1):
        passage_send("B", t)
    targets(ny, query_y(rest), 3)
    query_send("y", "B", half_y - 2)
    targets(nz, query_z, 2)
    targets(nz, query_z, 3)
    query_send("z", "A", half_z - 1)
    query_send("y", "A", half_y - 2)
    query_send("z", "B", half_z - 2)
    grad_z(1)
    for part in range(owned):
        s["co"][part] = block_sum(nx + 1, part).astype(jnp.bfloat16)
    core_reduce = send(s["co"], s["ci"], 12, s["got"].at[6], partner)
    start(core_reduce)
    query_send("y", "B", half_y - 3)
    for t in range(half_x - 1, 0, -1):
        passage_send("A", t)
    query_send("z", "A", half_z - 2)
    query_send("y", "A", half_y - 3)
    query_send("z", "B", half_z - 3)
    grad_z(0)
    grad_x(0, False)
    query_send("z", "A", half_z - 3)

    def arrived(line, n, device_at, parts, part):
        total = None
        for way in (0, 1):
            if n > 2 or (n == 2 and (way, part) in stream("A", parts)):
                reduce_copy(line, n, device_at, way, 1, part).wait_recv()
                value = came(line, n, way, 1, part)
                total = value if total is None else total + value
        return 0.0 if total is None else total

    core_reduce.wait_recv()
    for part in range(owned):
        s["own"][part] = block_sum(0, part) + block_sum(nx, part) + s["ci"][part].astype(jnp.float32)
    results = []
    for part in range(qp):
        block = pl.ds(part * piece, piece)
        value = s["gqy"][0, block, :] + s["gqz"][0, block, :]
        value += arrived("y", ny, at_y, qp, part)
        value += arrived("z", nz, at_z, qp, part)
        s["gqo"][part // CUTS, pl.ds(part % CUTS * piece, piece)] = value.astype(gq_ref.dtype)
    results.append(fetch(s["gqo"], gq_ref, 0))
    for part in range(owned):
        value = s["own"][part] + arrived("x", nx, at_x, owned, part)
        s["gpo"][part] = value.astype(gp_ref.dtype)
        results.append(fetch(s["gpo"].at[part], gp_ref.at[part], 1 + part))
    if ny > 1:
        for family, extent in ((0, s["yo"]), (9, s["yo"]), (7, s["ysr"].at[pl.ds(1, ny - 1)])):
            all_sent(family, extent)
    if nz > 1:
        for family, extent in ((1, s["zo"]), (10, s["zo"])):
            all_sent(family, extent)
        for family, extent in ((6, s["zsr"].at[pl.ds(1, nz - 1)]), (8, s["zfr"].at[pl.ds(1, nz - 1)])):
            all_sent(family, extent)
    if nx > 1:
        all_sent(2, s["xo"])
        all_sent(11, s["xo"])
    all_sent(3, s["pc"])
    all_sent(12, s["co"])
    for copy in results:
        copy.wait()


def hand_over(gq_in, gp_in, gq_out, gp_out, gq, gp, sems):
    pieces = [(gq_in, gq, gq_out, 0)] + [(gp_in, gp, gp_out, part) for part in range(gp_in.shape[0])]
    loads, stores = [], []
    for i, (src, held, dst, part) in enumerate(pieces):
        piece = slice(None) if i == 0 else pl.ds(part, 1)
        loads.append(pltpu.make_async_copy(src.at[piece], held.at[piece], sems.at[0, i]))
        stores.append(pltpu.make_async_copy(held.at[piece], dst.at[piece], sems.at[1, i]))
    for load in loads:
        load.start()
    for load, store in zip(loads, stores):
        load.wait()
        store.start()
    for store in stores:
        store.wait()


def solution(mesh, sizes=SIZES):
    nx, ny = sizes
    nz = mesh.shape["group"] // CORES
    assert mesh.shape["dp"] == nx * ny

    def shards(queries, passages, candidates, positives, row_weight, owner_map):
        listed = candidates.T
        plan = scratch_plan(nx, ny, nz, queries.shape[0], *passages.shape, listed.shape, owner_map.shape)
        left = pl.BlockSpec(memory_space=pl.ANY)
        shapes = (
            jax.ShapeDtypeStruct(queries.shape, queries.dtype),
            jax.ShapeDtypeStruct(passages.shape, passages.dtype),
        )
        results = pl.pallas_call(
            functools.partial(kernel, (nx, ny, nz), tuple(plan)),
            out_shape=shapes,
            in_specs=[left] * 6,
            out_specs=(left, left),
            scratch_shapes=list(plan.values()),
            compiler_params=pltpu.CompilerParams(
                collective_id=0, has_side_effects=True, vmem_limit_bytes=64_000_000
            ),
        )(queries, passages, listed, owner_map, positives, row_weight)
        return pl.pallas_call(
            hand_over,
            out_shape=shapes,
            in_specs=[left] * 2,
            out_specs=(left, left),
            scratch_shapes=[
                pltpu.VMEM(queries.shape, queries.dtype),
                pltpu.VMEM(passages.shape, passages.dtype),
                pltpu.SemaphoreType.DMA((2, passages.shape[0] + 1)),
            ],
        )(*results)

    return jax.shard_map(
        shards,
        mesh=mesh,
        in_specs=(
            P(("group", "dp"), None, None),
            P(("group", "dp"), None, None),
            P(),
            P(("group", "dp"), None),
            P(("group", "dp"), None),
            P(),
        ),
        out_specs=(P(("group", "dp"), None, None), P(("group", "dp"), None, None)),
        check_vma=False,
    )
```

```python
import functools
import math

import jax
import jax.numpy as jnp
from jax import lax
from jax.experimental import pallas as pl
from jax.experimental.pallas import tpu as pltpu
from jax.sharding import PartitionSpec as P

MESH = pl.DeviceIdType.MESH
NEG = -1e30
CORES = 2
CUTS = 2
SIZES = (4, 8)


def scratch_plan(nx, ny, nz, qb, owned, rows, width, cand_shape, map_shape):
    lanes, qp = qb * rows, qb * CUTS
    dma = pltpu.SemaphoreType.DMA
    bf, f32 = jnp.bfloat16, jnp.float32
    plan = {
        "qy": pltpu.VMEM((ny, lanes, width), bf),
        "qz": pltpu.VMEM((nz, lanes, width), bf),
        "pc": pltpu.VMEM((owned, rows, width), bf),
        "tab": pltpu.SMEM(((nx * ny + CORES * nz) * 3,), jnp.int32),
        "e": pltpu.VMEM((nx * ny + CORES * nz, rows, lanes), f32),
        "d": pltpu.VMEM((nx * ny + CORES * nz, rows, lanes), bf),
        "my": pltpu.VMEM((nx, ny, lanes), f32),
        "sy": pltpu.VMEM((nx, ny, lanes), f32),
        "mz": pltpu.VMEM((CORES, nz, lanes), f32),
        "sz": pltpu.VMEM((CORES, nz, lanes), f32),
        "zst": pltpu.VMEM((nz, lanes), f32),
        "zsr": pltpu.VMEM((nz, nz, lanes), f32),
        "yst": pltpu.VMEM((ny + 8, lanes), f32),
        "ysr": pltpu.VMEM((ny, ny + 8, lanes), f32),
        "ya": pltpu.VMEM((ny, lanes), f32),
        "fin": pltpu.VMEM((8, lanes), f32),
        "zfr": pltpu.VMEM((nz, 8, lanes), f32),
        "gqy": pltpu.VMEM((ny, lanes, width), f32),
        "gqz": pltpu.VMEM((nz, lanes, width), f32),
        "chain": pltpu.VMEM((nx + CORES, max(ny, nz) + 1, rows, width), f32),
        "own": pltpu.VMEM((owned, rows, width), f32),
        "yo": pltpu.VMEM((max(ny - 1, 1) * qp, lanes // qp, width), bf),
        "yi": pltpu.VMEM((max(ny - 1, 1) * qp, lanes // qp, width), bf),
        "zo": pltpu.VMEM((max(nz - 1, 1) * qp, lanes // qp, width), bf),
        "zi": pltpu.VMEM((max(nz - 1, 1) * qp, lanes // qp, width), bf),
        "xo": pltpu.VMEM((max(nx - 1, 1) * owned, rows, width), bf),
        "xi": pltpu.VMEM((max(nx - 1, 1) * owned, rows, width), bf),
        "co": pltpu.VMEM((owned, rows, width), bf),
        "ci": pltpu.VMEM((owned, rows, width), bf),
        "gqo": pltpu.VMEM((qb, rows, width), bf),
        "gpo": pltpu.VMEM((owned, rows, width), bf),
        "p0": pltpu.VMEM((owned, rows, width), bf),
        "cand": pltpu.SMEM(cand_shape, jnp.int32),
        "map": pltpu.SMEM(map_shape, jnp.int32),
        "posv": pltpu.VMEM((qb, rows), jnp.int32),
        "wv": pltpu.VMEM((qb, rows), f32),
        "links": pltpu.SMEM(((nx + CORES) * (max(ny, nz) + owned),), jnp.int32),
        "sent": dma((13,)),
        "got": dma((8,)),
        "near": dma((7,)),
        "yr": dma((max(ny - 1, 1) * qp,)),
        "zr": dma((max(nz - 1, 1) * qp,)),
        "xr": dma((max(nx - 1, 1) * owned,)),
        "xr2": dma((max(nx - 1, 1) * owned,)),
    }
    for h in range(1, nx):
        plan[f"px{h}"] = pltpu.VMEM((owned, rows, width), bf)
    return plan


def kernel(sizes, names, q_ref, p_ref, cand_ref, own_ref, pos_ref, w_ref, gq_ref, gp_ref, *scratch):
    nx, ny, nz = sizes
    s = dict(zip(names, scratch))
    qb, rows, width = q_ref.shape
    owned = p_ref.shape[0]
    ncand = cand_ref.shape[0]
    lanes, qp, piece = qb * rows, qb * CUTS, rows // CUTS
    scale = 3.0 / math.sqrt(width)
    dp_size = nx * ny
    g, dp = lax.axis_index("group"), lax.axis_index("dp")
    x, y = dp // ny, dp % ny
    z, c = g // CORES, g % CORES

    def at_y(r):
        return (g, x * ny + (y + r) % ny)

    def at_x(r):
        return (g, ((x + r) % nx) * ny + y)

    def at_z(r):
        return (((z + r) % nz) * CORES + c, dp)

    partner = (z * CORES + (1 - c), dp)

    peers = [at_y(r) for r in range(1, ny)] + [at_z(r) for r in range(1, nz)] + [partner]
    peers += [at_x(r) for r in sorted({1 % nx, (nx - 1) % nx} - {0})]
    def fetch(src, dst, sem):
        copy = pltpu.make_async_copy(src, dst, s["near"].at[sem])
        copy.start()
        return copy

    scalars = [fetch(cand_ref, s["cand"], 0), fetch(own_ref, s["map"], 1)]
    rows_in = [fetch(pos_ref, s["posv"], 2), fetch(w_ref, s["wv"], 3)]
    barrier = pltpu.get_barrier_semaphore()
    for peer in peers:
        pl.semaphore_signal(barrier, inc=1, device_id=peer, device_id_type=MESH)
    pl.semaphore_wait(barrier, len(peers))

    def send(src, dst, family, recv_sem, device):
        return pltpu.make_async_remote_copy(
            src_ref=src,
            dst_ref=dst,
            send_sem=s["sent"].at[family],
            recv_sem=recv_sem,
            device_id=device,
            device_id_type=MESH,
        )

    def start(copy):
        copy.start()

    def all_sent(family, extent):
        send(extent, extent, family, s["got"].at[7], partner).wait_send()

    def stream(kind, parts):
        return [
            (way, part)
            for part in range(parts)
            for way in (0, 1)
            if ((part >= parts // 2) == (way == 1)) == (kind == "A")
        ]

    def steps(n, kind):
        return n // 2 - (kind == "B")

    def slots(n, way, t):
        return ((-t) % n, (-(t + 1)) % n) if way == 0 else (t, t + 1)

    def entry(n, parts, way, t, part):
        half = n // 2
        return (2 * t + way) * parts + part if t < half - 1 else 2 * (half - 1) * parts + part

    def query_copy(line, n, device_at, way, t, part):
        src, dst = slots(n, way, t)
        buf = s["q" + line]
        block = pl.ds(part * piece, piece)
        return send(
            q_ref.at[part // CUTS, pl.ds(part % CUTS * piece, piece)] if t == 0 else buf.at[src, block],
            buf.at[dst, block],
            "yz".index(line),
            s[line + "r"].at[entry(n, qp, way, t, part)],
            device_at(1 if way == 0 else n - 1),
        )

    def y_copy(way, t, part):
        return query_copy("y", ny, at_y, way, t, part)

    def z_copy(way, t, part):
        return query_copy("z", nz, at_z, way, t, part)

    passages = [s["p0"]] + [s[f"px{h}"] for h in range(1, nx)]

    def x_copy(way, t, part):
        src, dst = slots(nx, way, t)
        return send(
            p_ref.at[part] if t == 0 else passages[src].at[part],
            passages[dst].at[part],
            2,
            s["xr"].at[entry(nx, owned, way, t, part)],
            at_x(1 if way == 0 else nx - 1),
        )

    rings = {"y": (ny, y_copy, qp), "z": (nz, z_copy, qp), "x": (nx, x_copy, owned)}

    def launch(line, kind, t):
        n, copy, parts = rings[line]
        if t < steps(n, kind):
            for way, part in stream(kind, parts):
                start(copy(way, t, part))

    def land(line, kind, t):
        n, copy, parts = rings[line]
        if t < steps(n, kind):
            for way, part in stream(kind, parts):
                copy(way, t, part).wait_recv()

    def relay(kind, t):
        for way, part in stream(kind, qp):
            for line in "yz":
                n, copy, _ = rings[line]
                if t - 1 < steps(n, kind):
                    copy(way, t - 1, part).wait_recv()
                if t < steps(n, kind):
                    start(copy(way, t, part))

    for kind in "AB":
        for line in "xyz":
            launch(line, kind, 0)
    core_gather = send(p_ref, s["pc"], 3, s["got"].at[0], partner)
    start(core_gather)

    whole_q = [fetch(q_ref.at[b], s["qy"].at[0, pl.ds(b * rows, rows)], 4 + b) for b in range(qb)]
    whole_p = fetch(p_ref, s["p0"], 4 + qb)
    for copy in rows_in:
        copy.wait()
    tile_row = lax.broadcasted_iota(jnp.int32, (8, lanes), 0)
    w_row = jnp.concatenate([s["wv"][b : b + 1, :] for b in range(qb)], axis=1) * scale
    pos_row = jnp.concatenate([s["posv"][b : b + 1, :] for b in range(qb)], axis=1).astype(jnp.float32)
    s["yst"][ny : ny + 8] = jnp.where(tile_row == 0, w_row, jnp.where(tile_row == 1, pos_row, 0.0))

    def spread(n, device_at, src, dst, family):
        for r in range(1, n):
            start(send(src, dst.at[n - r], family, s["got"].at[family - 3], device_at(r)))

        def wait():
            if n > 1:
                extent = dst.at[pl.ds(1, n - 1)]
                send(extent, extent, family, s["got"].at[family - 3], partner).wait_recv()

        return wait

    def entry_y(h, r):
        return (h * ny + r) * 3

    def entry_z(h, r):
        return (nx * ny + h * nz + r) * 3

    def fill(lister, holders, entries):
        found = [jnp.int32(0)] * len(holders)
        for b in range(qb):
            listing = [jnp.int32(-1)] * len(holders)
            for k in range(ncand):
                place = s["map"][s["cand"][k, lister * qb + b]]
                for i, holder in enumerate(holders):
                    offset = place - holder * owned
                    hit = offset.astype(jnp.uint32) < jnp.uint32(owned)
                    listing[i] = jnp.where(hit, k, listing[i])
                    found[i] = jnp.where(hit, offset, found[i])
            for i, entry in enumerate(entries):
                s["tab"][entry + b] = listing[i]
        for i, entry in enumerate(entries):
            s["tab"][entry + 2] = found[i]

    def fill_y(r, carry):
        holders = [g * dp_size + ((x + h) % nx) * ny + y for h in range(nx)]
        fill(g * dp_size + x * ny + (y + r) % ny, holders, [entry_y(h, r) for h in range(nx)])
        return carry

    def fill_z(r, carry):
        own = jnp.where(r == 0, -1000, g * dp_size + dp)
        other = (z * CORES + (1 - c)) * dp_size + dp
        fill((((z + r) % nz) * CORES + c) * dp_size + dp, [own, other], [entry_z(h, r) for h in range(CORES)])
        return carry

    for copy in scalars:
        copy.wait()
    lax.fori_loop(0, nz, fill_z, 0)
    for copy in whole_q:
        copy.wait()
    s["qz"][0] = s["qy"][0]
    whole_p.wait()

    lane = lax.broadcasted_iota(jnp.int32, (1, lanes), 1)

    def listing_row(entry):
        row = jnp.full((1, lanes), s["tab"][entry], jnp.int32)
        for b in range(1, qb):
            row = jnp.where(lane >= b * rows, s["tab"][entry + b], row)
        return row

    def score(pairs, q):
        blocks = [held[s["tab"][where + 2]] for held, where, _, _, _ in pairs]
        block = jnp.concatenate(blocks, axis=0) if len(blocks) > 1 else blocks[0]
        joined = lax.dot_general(block, q, (((1,), (1,)), ((), ())), preferred_element_type=jnp.float32) * scale
        for i, (_, where, index, (top_ref, lse_ref, h), r) in enumerate(pairs):
            scores = joined[i * rows : (i + 1) * rows]
            scores = jnp.where(listing_row(where) >= 0, scores, NEG)
            top = jnp.max(scores, axis=0, keepdims=True)
            powers = jnp.exp(scores - top)
            s["e"][index] = powers
            top_ref[h, pl.ds(r, 1), :] = top
            lse_ref[h, pl.ds(r, 1), :] = top + jnp.log(jnp.sum(powers, axis=0, keepdims=True))

    def score_y(hs, r):
        score([(passages[h], entry_y(h, r), h * ny + r, (s["my"], s["sy"], h), r) for h in hs], s["qy"][r])

    held_z = [s["p0"], s["pc"]]

    def score_z(r):
        pairs = [(held_z[h], entry_z(h, r), nx * ny + h * nz + r, (s["mz"], s["sz"], h), r) for h in range(CORES)]
        score(pairs, s["qz"][r])

    def each(count, first_slot, n, body):
        def step(i, carry):
            body((i + first_slot) % n)
            return carry

        lax.fori_loop(0, count, step, 0)

    half_y, half_z, half_x = ny // 2, nz // 2, nx // 2
    near_y, near_z = max(half_y - 2, 0), max(half_z - 2, 0)
    relay("A", 1)
    lax.fori_loop(0, ny // 2, fill_y, 0)
    relay("B", 1)
    lax.fori_loop(ny // 2, ny, fill_y, 0)
    for t in range(1, half_x):
        land("x", "A", t - 1)
        launch("x", "A", t)
    relay("A", 2)

    span = max(ny, nz) + owned
    for h in range(nx + CORES):
        n = ny if h < nx else nz
        found = [s["tab"][(entry_y(h, r) if h < nx else entry_z(h - nx, r)) + 2] for r in range(n)]
        for r in range(n):
            before = jnp.int32(0)
            for other in range(r):
                before = jnp.where(found[other] == found[r], other + 1, before)
            s["links"][h * span + r] = before
        for p in range(owned):
            last = jnp.int32(0)
            for r in range(n):
                last = jnp.where(found[r] == p, r + 1, last)
            s["links"][h * span + max(ny, nz) + p] = last
        s["chain"][h, 0] = jnp.zeros((rows, width), jnp.float32)

    relay("B", 2)
    core_gather.wait_recv()
    each(2 * near_z + 1, nz - near_z, nz, score_z)
    relay("A", 3)
    each(2 * near_y + 1, ny - near_y, ny, lambda r: score_y([0], r))
    relay("B", 3)
    relay("A", 4)
    each(nz - 2 * near_z - 1, near_z + 1, nz, score_z)

    def merge(parts):
        top = functools.reduce(jnp.maximum, parts)
        return top + jnp.log(sum(jnp.exp(part - top) for part in parts))

    s["zst"][...] = merge([s["sz"][h] for h in range(CORES)])
    stat_z = spread(nz, at_z, s["zst"], s["zsr"], 6)
    each(ny - 2 * near_y - 1, near_y + 1, ny, lambda r: score_y([0], r))

    for t in range(half_x - 1):
        land("x", "B", t)
    middle = [h for h in range(1, nx) if h != half_x]

    if middle:
        each(ny, 0, ny, lambda r: score_y(middle, r))
    own_z = [s["zst"][0:1, :]]
    stat_z()
    own_z += [s["zsr"][j][nz - j : nz - j + 1, :] for j in range(1, nz)]
    z_row = merge(own_z)
    if nx > 1:
        land("x", "A", half_x - 1)

        def last_pairs(i):
            score_y([half_x], i)
            score_y([half_x], i + ny // 2)

        each(ny // 2, 0, ny, last_pairs)

    stat = merge([s["sy"][h] for h in range(nx)])
    ring_row = lax.broadcasted_iota(jnp.int32, (ny, lanes), 0)
    stat = jnp.where(ring_row == 0, merge([stat, jnp.broadcast_to(z_row, stat.shape)]), stat)
    s["yst"][0:ny] = stat
    stat_y = spread(ny, at_y, s["yst"], s["ysr"], 7)
    stat_y()

    def turned(value, places):
        if ny == 8:
            return pltpu.roll(value, places, axis=0)
        return jnp.concatenate([value[ny - places :], value[: ny - places]], axis=0)

    total = merge([stat] + [turned(s["ysr"][j, 0:ny], j) for j in range(1, ny)])
    s["ya"][...] = total
    w_row, pos_row = s["yst"][ny : ny + 1, :], s["yst"][ny + 1 : ny + 2, :]
    fin = jnp.where(tile_row == 1, w_row, jnp.where(tile_row == 2, pos_row, 0.0))
    s["fin"][...] = jnp.where(tile_row == 0, total[0:1, :], fin)
    fin_z = spread(nz, at_z, s["fin"], s["zfr"], 8)

    s["ysr"][0] = s["yst"][...]

    down = lax.broadcasted_iota(jnp.int32, (rows, lanes), 0).astype(jnp.float32)

    def dscore(index, entry, m_row, a_row, w_line, pos_line):
        factor = jnp.exp(m_row - a_row) * w_line
        spot = pos_line - (listing_row(entry) * rows).astype(jnp.float32)
        value = s["e"][index] * factor - jnp.where(down == spot, w_line, 0.0)
        s["d"][index] = value.astype(jnp.bfloat16)

    def dscore_y(h, r):
        dscore(
            h * ny + r,
            entry_y(h, r),
            s["my"][h, pl.ds(r, 1), :],
            s["ya"][pl.ds(r, 1), :],
            s["ysr"][r, ny : ny + 1, :],
            s["ysr"][r, ny + 1 : ny + 2, :],
        )

    def dscore_z(h, r, a_row):
        dscore(
            nx * ny + h * nz + r,
            entry_z(h, r),
            s["mz"][h, pl.ds(r, 1), :],
            a_row,
            s["zfr"][r, 1:2, :],
            s["zfr"][r, 2:3, :],
        )

    def term(h, r, index, q):
        value = jnp.dot(s["d"][index], q, preferred_element_type=jnp.float32)
        s["chain"][h, r + 1] = value + s["chain"][h, s["links"][h * span + r]]

    def block_sum(h, p):
        return s["chain"][h, s["links"][h * span + max(ny, nz) + p]]

    def query_part(out, r, pairs):
        left = jnp.concatenate([s["d"][index] for index, _, _ in pairs], axis=0)
        right = jnp.concatenate([held[s["tab"][where + 2]] for _, held, where in pairs], axis=0)
        out[r] = lax.dot_general(left, right, (((0,), (0,)), ((), ())), preferred_element_type=jnp.float32)

    def reduce_copy(line, n, device_at, way, t, part):
        place = entry(n, owned if line == "x" else qp, way, t - 1, part)
        return send(
            s[line + "o"].at[place],
            s[line + "i"].at[place],
            9 + "yzx".index(line),
            s["xr2" if line == "x" else line + "r"].at[place],
            device_at(1 if way == 0 else n - 1),
        )

    def came(line, n, way, t, part):
        return s[line + "i"][entry(n, owned if line == "x" else qp, way, t - 1, part)].astype(jnp.float32)

    def reduce_send(line, n, device_at, way, t, part, value, alone):
        if not alone:
            reduce_copy(line, n, device_at, way, t + 1, part).wait_recv()
            value = value + came(line, n, way, t + 1, part)
        s[line + "o"][entry(n, owned if line == "x" else qp, way, t - 1, part)] = value.astype(jnp.bfloat16)
        start(reduce_copy(line, n, device_at, way, t, part))

    def query_send(line, kind, t):
        n, device_at = (ny, at_y) if line == "y" else (nz, at_z)
        if 1 <= t <= steps(n, kind):
            for way, part in stream(kind, qp):
                target = t if way == 0 else (n - t) % n
                value = s["gq" + line][target, pl.ds(part * piece, piece), :]
                reduce_send(line, n, device_at, way, t, part, value, t == steps(n, kind))

    def passage_send(kind, t):
        if 1 <= t <= steps(nx, kind):
            for way, part in stream(kind, owned):
                target = t if way == 0 else (nx - t) % nx
                reduce_send("x", nx, at_x, way, t, part, block_sum(target, part), t == steps(nx, kind))

    def grad_x(h, fresh):
        def pair(r):
            if fresh:
                dscore_y(h, r)
            term(h, r, h * ny + r, s["qy"][r])

        each(ny, 0, ny, pair)

    if nx > 1:
        grad_x(half_x, True)
        passage_send("A", half_x)
    rest = [h for h in range(nx) if nx == 1 or h != half_x]

    def query_y(hs):
        def body(r):
            for h in hs:
                dscore_y(h, r)
            query_part(s["gqy"], r, [(h * ny + r, passages[h], entry_y(h, r)) for h in range(nx)])

        return body

    def query_z(r):
        a_row = s["zfr"][r, 0:1, :]
        for h in range(CORES):
            dscore_z(h, r, a_row)
        query_part(s["gqz"], r, [(nx * ny + h * nz + r, held_z[h], entry_z(h, r)) for h in range(CORES)])

    def grad_z(h):
        each(nz, 0, nz, lambda r: term(nx + h, r, nx * ny + h * nz + r, s["qz"][r]))

    def targets(n, body, group):
        half = n // 2
        if group == 0:
            each(1, half, n, body)
        elif group == 3 and n > 1:
            each(min(3, n - 1), n - 1 if n > 2 else 0, n, body)
        elif group in (1, 2) and n > 2:
            each(2, 0, 2, lambda i: body(half - group + 2 * group * i))

    assert ny in (1, 2, 8) and nz in (1, 2, 8)
    targets(ny, query_y(rest), 0)
    query_send("y", "A", half_y)
    for h in middle[:1]:
        grad_x(h, True)
    rest = [h for h in rest if h not in middle[:1]]
    targets(ny, query_y(rest), 1)
    query_send("y", "B", half_y - 1)
    for h in middle[1:]:
        grad_x(h, True)
    rest = [h for h in rest if h not in middle]
    targets(ny, query_y(rest), 2)
    fin_z()
    s["zfr"][0] = s["fin"][...]
    targets(nz, query_z, 0)
    query_send("z", "A", half_z)
    query_send("y", "A", half_y - 1)
    targets(nz, query_z, 1)
    query_send("z", "B", half_z - 1)
    for t in range(half_x - 1, 0, -1):
        passage_send("B", t)
    targets(ny, query_y(rest), 3)
    query_send("y", "B", half_y - 2)
    targets(nz, query_z, 2)
    targets(nz, query_z, 3)
    query_send("z", "A", half_z - 1)
    query_send("y", "A", half_y - 2)
    query_send("z", "B", half_z - 2)
    grad_z(1)
    for part in range(owned):
        s["co"][part] = block_sum(nx + 1, part).astype(jnp.bfloat16)
    core_reduce = send(s["co"], s["ci"], 12, s["got"].at[6], partner)
    start(core_reduce)
    query_send("y", "B", half_y - 3)
    for t in range(half_x - 1, 0, -1):
        passage_send("A", t)
    query_send("z", "A", half_z - 2)
    query_send("y", "A", half_y - 3)
    query_send("z", "B", half_z - 3)
    grad_z(0)
    grad_x(0, False)
    query_send("z", "A", half_z - 3)

    def arrived(line, n, device_at, parts, part):
        total = None
        for way in (0, 1):
            if n > 2 or (n == 2 and (way, part) in stream("A", parts)):
                reduce_copy(line, n, device_at, way, 1, part).wait_recv()
                value = came(line, n, way, 1, part)
                total = value if total is None else total + value
        return 0.0 if total is None else total

    core_reduce.wait_recv()
    for part in range(owned):
        s["own"][part] = block_sum(0, part) + block_sum(nx, part) + s["ci"][part].astype(jnp.float32)
    results = []
    for part in range(qp):
        block = pl.ds(part * piece, piece)
        value = s["gqy"][0, block, :] + s["gqz"][0, block, :]
        value += arrived("y", ny, at_y, qp, part)
        value += arrived("z", nz, at_z, qp, part)
        s["gqo"][part // CUTS, pl.ds(part % CUTS * piece, piece)] = value.astype(gq_ref.dtype)
    results.append(fetch(s["gqo"], gq_ref, 0))
    for part in range(owned):
        value = s["own"][part] + arrived("x", nx, at_x, owned, part)
        s["gpo"][part] = value.astype(gp_ref.dtype)
        results.append(fetch(s["gpo"].at[part], gp_ref.at[part], 1 + part))
    if ny > 1:
        for family, extent in ((0, s["yo"]), (9, s["yo"]), (7, s["ysr"].at[pl.ds(1, ny - 1)])):
            all_sent(family, extent)
    if nz > 1:
        for family, extent in ((1, s["zo"]), (10, s["zo"])):
            all_sent(family, extent)
        for family, extent in ((6, s["zsr"].at[pl.ds(1, nz - 1)]), (8, s["zfr"].at[pl.ds(1, nz - 1)])):
            all_sent(family, extent)
    if nx > 1:
        all_sent(2, s["xo"])
        all_sent(11, s["xo"])
    all_sent(3, s["pc"])
    all_sent(12, s["co"])
    for copy in results:
        copy.wait()


def hand_over(gq_in, gp_in, gq_out, gp_out, gq, gp, sems):
    pieces = [(gq_in, gq, gq_out, 0)] + [(gp_in, gp, gp_out, part) for part in range(gp_in.shape[0])]
    loads, stores = [], []
    for i, (src, held, dst, part) in enumerate(pieces):
        piece = slice(None) if i == 0 else pl.ds(part, 1)
        loads.append(pltpu.make_async_copy(src.at[piece], held.at[piece], sems.at[0, i]))
        stores.append(pltpu.make_async_copy(held.at[piece], dst.at[piece], sems.at[1, i]))
    for load in loads:
        load.start()
    for load, store in zip(loads, stores):
        load.wait()
        store.start()
    for store in stores:
        store.wait()


def solution(mesh, sizes=SIZES):
    nx, ny = sizes
    nz = mesh.shape["group"] // CORES
    assert mesh.shape["dp"] == nx * ny

    def shards(queries, passages, candidates, positives, row_weight, owner_map):
        listed = candidates.T
        plan = scratch_plan(nx, ny, nz, queries.shape[0], *passages.shape, listed.shape, owner_map.shape)
        left = pl.BlockSpec(memory_space=pl.ANY)
        shapes = (
            jax.ShapeDtypeStruct(queries.shape, queries.dtype),
            jax.ShapeDtypeStruct(passages.shape, passages.dtype),
        )
        results = pl.pallas_call(
            functools.partial(kernel, (nx, ny, nz), tuple(plan)),
            out_shape=shapes,
            in_specs=[left] * 6,
            out_specs=(left, left),
            scratch_shapes=list(plan.values()),
            compiler_params=pltpu.CompilerParams(
                collective_id=0, has_side_effects=True, vmem_limit_bytes=64_000_000
            ),
        )(queries, passages, listed, owner_map, positives, row_weight)
        return pl.pallas_call(
            hand_over,
            out_shape=shapes,
            in_specs=[left] * 2,
            out_specs=(left, left),
            scratch_shapes=[
                pltpu.VMEM(queries.shape, queries.dtype),
                pltpu.VMEM(passages.shape, passages.dtype),
                pltpu.SemaphoreType.DMA((2, passages.shape[0] + 1)),
            ],
        )(*results)

    return jax.shard_map(
        shards,
        mesh=mesh,
        in_specs=(
            P(("group", "dp"), None, None),
            P(("group", "dp"), None, None),
            P(),
            P(("group", "dp"), None),
            P(("group", "dp"), None),
            P(),
        ),
        out_specs=(P(("group", "dp"), None, None), P(("group", "dp"), None, None)),
        check_vma=False,
    )
```
